32 devices in a mesh: lat: 8 (over y, x, core), lon: 4 (over z).
Axes of the slice: x: 2, y: 2, z: 4, core: 2. Of those that a mesh axis runs over, the one named last changes fastest.
Arguments:
- adjoint: float32 [8, 8, 256, 512], P(None, None, 'lat', 'lon'), may hold values from -6 to 6
- transport: float32 [6, 8, 256, 512], P(None, None, 'lat', 'lon'), may hold values from 0.03 to 0.14
- cell_weight: float32 [256, 512], P('lat', 'lon'), may hold values from 0.1 to 1
- region_local: int32 [256, 512], P('lat', 'lon'), may hold values from 0 to 255
- tile_regions: int32 [32, 256], replicated, may hold values from 0 to 2047, as said below
- polar_rows: int32 [256], P('lat'), may hold values 0 or 1
- week_index: int32 [1], replicated, may hold values from 0 to 51
- grad_in: bfloat16 [2048, 416], P(('lat', 'lon')), may hold values from -6 to 6
- covariance: bfloat16 [2048, 2048], P(('lat', 'lon')), may hold values from -0.25 to 0.25
Outputs:
- adjoint_out: float32 [8, 8, 256, 512], P(None, None, 'lat', 'lon')
- precond: float32 [2048, 416], P(('lat', 'lon'))
The draws below stay inside these ranges and needn't reach their ends.
Inputs may be any that keep to these rules, and one draw needn't show every extreme that they name: `tile_regions`: each row holds 256 different region numbers; with per = 8, entries o * per to o * per + per - 1 of a row lie in regions o * 64 to o * 64 + 63, for every o.
All inputs are finite; a program needn't handle non-finite values. No bound on the sum of `polar_rows` on one device may be relied on, other than what follows from the above.
Results may differ from the reference program's by a relative error of at most 0.00066.
Values may be sent and summed in bfloat16 or wider, within the bound.
No kernel may reach another device: no remote copies, remote signals or barrier semaphores. Data moves between devices by JAX's collectives and lax.ppermute only.
A program may use at most 128 MiB of HBM per device.

```python
import math
import jax
import jax.numpy as jnp

TRC = 8
LEV = 8
CLAT = 32
CLON = 128
LOCAL = 256
REG_DEV = 64
WEEKS = 52
NLAT = 256
NLON = 512
TILES = 32
REGIONS = 2048
N_LON = 4


def draw_tile_regions(key, part):
    per_owner = LOCAL // TILES
    scores = jax.random.randint(jax.random.fold_in(key, 11), (TILES, TILES, REG_DEV), 0, 1048576, dtype=jnp.int32)
    scores = scores * REG_DEV + jnp.arange(REG_DEV, dtype=jnp.int32)[None, None, :]
    picked = jnp.argsort(scores, axis=2, stable=True)[:, :, :per_owner].astype(jnp.int32)
    offsets = (jnp.arange(TILES, dtype=jnp.int32) * REG_DEV)[None, :, None]
    return (picked + offsets).reshape(TILES, LOCAL).astype(jnp.int32)


def plant(result, rng, smallest, top_value):
    index_at = [jax.random.randint(jax.random.fold_in(rng, axis), (), 0, length) for axis, length in enumerate(result.shape)]
    widest = result.shape.index(max(result.shape))
    next_to = index_at[:widest] + [(index_at[widest] + 1) % result.shape[widest]] + index_at[widest + 1:]
    return result.at[tuple(index_at)].set(smallest).at[tuple(next_to)].set(top_value)


def spiked(values, rng, source, target, blocks, factor):
    owner, partner = [(jnp.arange(values.shape[axis_at]) // (values.shape[axis_at] // blocks)).reshape([-1 if axis == axis_at else 1 for axis in range(values.ndim)]) for axis_at in (source, target)]
    chosen = jax.random.permutation(rng, blocks)[partner]
    strong = (owner == chosen) | (owner == (partner + blocks // 2) % blocks)
    return jnp.where(strong, factor * values, values)


def block_levels(stream_key, extent, pieces, low, top_value):
    def one(position, blocks):
        draws = jax.random.uniform(jax.random.fold_in(jax.random.fold_in(stream_key, 6), position), (blocks,), jnp.float32, low / len(pieces), top_value / len(pieces))
        return jnp.repeat(jnp.exp(draws), extent[position] // blocks).reshape((-1,) + (1,) * (len(extent) - position - 1))

    level = one(*pieces[0])
    for cut in pieces[1:]:
        level = level * one(*cut)
    return level


def gaussian(rng, shape, spread, bound, split=(), kind=jnp.bfloat16):
    drawn = jax.random.normal(rng, shape, jnp.float32) * spread
    if len(split) > 0:
        drawn = block_levels(rng, shape, split, -0.22, 0.18) * drawn
    return jnp.clip(drawn, min=-bound, max=bound).astype(kind)


def bell_draw_with(own_key, shape, deviation, bound, pieces, heavy, kind=jnp.bfloat16):
    drawn = deviation * jax.random.normal(own_key, shape, jnp.float32)
    if pieces:
        drawn = drawn * block_levels(own_key, shape, pieces, -0.22, 0.18)
    return jnp.clip(spiked(drawn, jax.random.fold_in(own_key, 3), *heavy), -bound, bound).astype(kind)


def setup_inputs(seed: int = 0) -> dict:
    key_list = jax.random.split(jax.random.key(seed), 10)
    return {
        "adjoint": gaussian(key_list[0], (TRC, LEV, NLAT, NLON), 1.0, 6.0, ((2, 8), (3, 4)), jnp.float32),
        "transport": jnp.clip(0.03 + 0.11 * jax.random.uniform(key_list[1], (6, LEV, NLAT, NLON), jnp.float32) ** block_levels(key_list[1], (6, LEV, NLAT, NLON), ((2, 8), (3, 4)), -0.2, 0.2), 0.03, 0.14),
        "cell_weight": jnp.clip(jnp.exp(math.log(1.0) - 2.3025851 * jax.random.uniform(key_list[2], (NLAT, NLON), jnp.float32) ** block_levels(key_list[2], (NLAT, NLON), ((0, 8), (1, 4)), -0.2, 0.2)), 0.1, 1.0),
        "region_local": plant(jax.random.randint(key_list[3], (NLAT, NLON), 0, LOCAL), jax.random.fold_in(key_list[3], 1), 0, LOCAL - 1).astype(jnp.int32),
        "tile_regions": draw_tile_regions(jax.random.fold_in(key_list[9], 71), 0),
        "polar_rows": plant((jax.random.randint(key_list[5], (NLAT,), 0, 4) < 1).astype(jnp.int32), jax.random.fold_in(key_list[5], 1), 0, 1),
        "week_index": jax.random.randint(key_list[6], (1,), 0, WEEKS).astype(jnp.int32),
        "grad_in": gaussian(key_list[7], (REGIONS, WEEKS * TRC), 1.0, 6.0, ((0, 32),)),
        "covariance": bell_draw_with(key_list[8], (REGIONS, REGIONS), REGIONS ** -0.5, 0.25, ((0, 32),), (1, 0, 32, 2.75)),
    }


def advance(field, rates):
    wrapped = jnp.concatenate([field[..., -1:], field, field[..., :1]], axis=3)
    padded = jnp.pad(wrapped, ((0, 0), (0, 0), (1, 1), (0, 0)))
    centre = padded[:, :, 1:-1, 1:-1]
    to_east = padded[:, :, 1:-1, 2:] - centre
    to_west = padded[:, :, 1:-1, :-2] - centre
    to_north = padded[:, :, 2:, 1:-1] - centre
    to_south = padded[:, :, :-2, 1:-1] - centre
    flat_zero = jnp.zeros_like(centre[:, :1])
    upper = jnp.concatenate([centre[:, 1:] - centre[:, :-1], flat_zero], axis=1)
    lower = jnp.concatenate([flat_zero, centre[:, :-1] - centre[:, 1:]], axis=1)
    return (centre + rates[0] * to_east + rates[1] * to_west + rates[2] * to_north
            + rates[3] * to_south + rates[4] * upper + rates[5] * lower)


def reference(adjoint, transport, cell_weight, region_local, tile_regions, polar_rows, week_index, grad_in, covariance):
    field = advance(advance(adjoint, transport), transport)
    zonal = jnp.mean(field, axis=3, keepdims=True)
    flags = polar_rows.astype(jnp.float32)[None, None, :, None]
    adjoint_out = field + 0.5 * flags * (zonal - field)
    surface = adjoint_out[:, 0] * cell_weight[None]
    row_ids = jnp.arange(NLAT, dtype=jnp.int32) // CLAT
    col_ids = jnp.arange(NLON, dtype=jnp.int32) // CLON
    tile_ids = row_ids[:, None] * N_LON + col_ids[None, :]
    gid = tile_regions[tile_ids, region_local]
    fresh = jnp.zeros((REGIONS, TRC), jnp.float32).at[gid.reshape(-1)].add(surface.reshape(TRC, -1).T)
    fresh = fresh.astype(jnp.bfloat16)
    base = jnp.dot(covariance, grad_in, preferred_element_type=jnp.float32)
    added = jnp.dot(covariance, fresh, preferred_element_type=jnp.float32)
    week_hot = (jnp.arange(WEEKS, dtype=jnp.int32) == week_index[0]).astype(jnp.float32)
    precond = base.reshape(REGIONS, WEEKS, TRC) + week_hot[None, :, None] * added[:, None, :]
    return adjoint_out, precond.reshape(REGIONS, WEEKS * TRC)
```

```python
import functools
import math

import jax
import jax.numpy as jnp
from jax import lax
from jax.experimental import pallas as pl
from jax.experimental.pallas import tpu as pltpu
from jax.sharding import PartitionSpec as P

AXES = ("lat", "lon")
F32 = jnp.float32
BF16 = jnp.bfloat16
LANES = 128
OFF = 8
VMEM = pl.BlockSpec(memory_space=pltpu.VMEM)
SMEM = pl.BlockSpec(memory_space=pltpu.SMEM)
HBM = pl.BlockSpec(memory_space=pl.ANY)


def iota(shape, dim):
    return lax.broadcasted_iota(jnp.int32, shape, dim)


BIG = 4 << 20


def nbytes(shape, dtype):
    return math.prod(shape) * jnp.dtype(dtype).itemsize


def call(body, outs, in_specs, scratch=(), aliases=None, keep=True):
    def placed(s, d):
        return pltpu.VMEM(s, d) if keep and nbytes(s, d) <= BIG else jax.ShapeDtypeStruct(s, d)

    def apply(*args):
        own = sum(nbytes(x.shape, x.dtype) for x in scratch if x.memory_space == pltpu.VMEM)
        own += sum(nbytes(x.shape, x.dtype) for x in args if nbytes(x.shape, x.dtype) > BIG)
        own += sum(nbytes(s, d) for s, d in outs if not keep or nbytes(s, d) > BIG)
        run = pl.pallas_call(
            body,
            out_shape=[placed(s, d) for s, d in outs],
            in_specs=in_specs,
            out_specs=[VMEM] * len(outs),
            scratch_shapes=list(scratch),
            input_output_aliases=aliases or {},
            compiler_params=pltpu.CompilerParams(vmem_limit_bytes=own + (6 << 20)),
        )
        return run(*(pltpu.with_memory_space_constraint(x, pltpu.VMEM)
                     if spec is VMEM and nbytes(x.shape, x.dtype) <= BIG else x
                     for x, spec in zip(args, in_specs)))

    return apply


def split3(x):
    hi = x.astype(BF16).astype(F32)
    rest = x - hi
    mid = rest.astype(BF16).astype(F32)
    return hi, mid, rest - mid


def rows_kernel(trc, lev, f_last, f_first, t_last, t_first, up, down):
    def row(ref, group, at):
        return ref[pl.ds(group * lev * 8 + at, lev, stride=8), :]

    for k in range(trc):
        up[k] = row(f_last, k, 6)
        up[trc + k] = row(f_last, k, 7)
        down[k] = row(f_first, k, 1)
        down[trc + k] = row(f_first, k, 0)
    for d in range(6):
        up[2 * trc + d] = row(t_last, d, 7)
        down[2 * trc + d] = row(t_first, d, 0)


def border_rows(field, rates):
    trc, lev, rows, _ = field.shape
    last = rows // 8 - 1

    def body(f_last, f_first, t_last, t_first, up, down):
        flat = lambda ref: ref.reshape(ref.shape[0] * 8, LANES)
        rows_kernel(trc, lev, flat(f_last), flat(f_first), flat(t_last), flat(t_first), up, down)

    f3 = field.reshape(trc * lev, rows, LANES)
    t3 = rates.reshape(6 * lev, rows, LANES)
    out = pltpu.VMEM((2 * trc + 6, lev, LANES), F32)
    return pl.pallas_call(
        body,
        grid=(1,),
        out_shape=[out, out],
        in_specs=[
            pl.BlockSpec((trc * lev, 8, LANES), lambda i: (0, last, 0)),
            pl.BlockSpec((trc * lev, 8, LANES), lambda i: (0, 0, 0)),
            pl.BlockSpec((6 * lev, 8, LANES), lambda i: (0, last, 0)),
            pl.BlockSpec((6 * lev, 8, LANES), lambda i: (0, 0, 0)),
        ],
        out_specs=[VMEM] * 2,
        compiler_params=pltpu.CompilerParams(vmem_limit_bytes=8 << 20),
        name="border_rows",
    )(f3, f3, t3, t3)


def border_cols(field, rates):
    trc, lev, rows, _ = field.shape
    tiles = trc * lev

    def body(f, t, east, west):
        lane = iota((8, LANES), 1)
        east[pl.ds(2 * rows, 8), :] = jnp.zeros((8, LANES), F32)
        west[pl.ds(2 * rows, 8), :] = jnp.zeros((8, LANES), F32)
        for c in range(0, rows, 8):
            e = jnp.zeros((8, LANES), F32)
            w = jnp.zeros((8, LANES), F32)
            for m in range(tiles):
                v = f[m, pl.ds(c, 8), :]
                e = jnp.where(lane == m, pltpu.roll(v, (m - 127) % LANES, 1), e)
                e = jnp.where(lane == 64 + m, pltpu.roll(v, (64 + m - 126) % LANES, 1), e)
                w = jnp.where(lane == m, pltpu.roll(v, m % LANES, 1), w)
                w = jnp.where(lane == 64 + m, pltpu.roll(v, (64 + m - 1) % LANES, 1), w)
            east[pl.ds(c, 8), :] = e
            west[pl.ds(c, 8), :] = w
            e = jnp.zeros((8, LANES), F32)
            w = jnp.zeros((8, LANES), F32)
            for j in range(6 * lev):
                v = t[j, pl.ds(c, 8), :]
                e = jnp.where(lane == j, pltpu.roll(v, (j - 127) % LANES, 1), e)
                w = jnp.where(lane == j, pltpu.roll(v, j % LANES, 1), w)
            east[pl.ds(rows + c, 8), :] = e
            west[pl.ds(rows + c, 8), :] = w

    return call(body, [((2 * rows + 8, LANES), F32)] * 2, [VMEM, VMEM])(
        field.reshape(tiles, rows, LANES), rates.reshape(6 * lev, rows, LANES))


def masks(band, bands):
    south = jnp.where(band > 0, 1.0, 0.0).astype(F32)
    north = jnp.where(band < bands - 1, 1.0, 0.0).astype(F32)
    return south, north


def corners(east, west, before, after, band, bands):
    rows = (east.shape[0] - 8) // 2
    lev = before.shape[1]
    trc = (before.shape[0] - 6) // 2

    def body(band_ref, east_in, west_in, b, a, e_ref, w_ref):
        lane, sub = iota((lev, LANES), 1), iota((lev, LANES), 0)
        e_ref[...] = east_in[...]
        w_ref[...] = west_in[...]
        for which, (ref, mask) in enumerate(zip((b, a), masks(band_ref[0], bands))):
            to_e = jnp.zeros((lev, LANES), F32)
            to_w = jnp.zeros((lev, LANES), F32)
            for k in range(trc):
                v = ref[trc + k] * mask
                here = lane == k * lev + sub
                to_e = jnp.where(here, jnp.broadcast_to(v[:, LANES - 1 :], v.shape), to_e)
                to_w = jnp.where(here, jnp.broadcast_to(v[:, :1], v.shape), to_w)
            e_ref[pl.ds(2 * rows + which, 1), :] = jnp.sum(to_e, axis=0, keepdims=True)
            w_ref[pl.ds(2 * rows + which, 1), :] = jnp.sum(to_w, axis=0, keepdims=True)

    return call(body, [(x.shape, F32) for x in (east, west)], [SMEM] + [VMEM] * 4)(
        band, east, west, before, after)


def transport_kernel(trc, lev, rows, bands, band_ref, field, tv, w_in, e_in, my_east, my_west, b, a, my_up, my_down,
                     lam, level0, row_sums, f1, cols, gw, ge):
    high = rows + 2 * OFF
    lane = iota((8, LANES), 1)
    sub = iota((lev, LANES), 0)
    lane_l = iota((lev, LANES), 1)
    f0 = field.reshape(trc * lev * rows, LANES)
    bf, af = (x.reshape((2 * trc + 6) * lev, LANES) for x in (b, a))
    south_mask, north_mask = masks(band_ref[0], bands)
    edge = iota((8, LANES), 0)
    tvf = tv.reshape(6 * lev * rows, LANES)
    lamf = lam.reshape(trc * lev * rows, LANES)
    for which, (ref, mine, mask) in enumerate(zip((b, a), (my_down, my_up), masks(band_ref[0], bands))):
        rate = [ref[2 * trc + d] for d in range(6)]
        rate[4] = jnp.where(sub < lev - 1, rate[4], 0.0)
        rate[5] = jnp.where(sub > 0, rate[5], 0.0)
        mid = 1.0 - rate[0] - rate[1] - rate[2] - rate[3] - rate[4] - rate[5]
        west_corner = jnp.broadcast_to(w_in[pl.ds(2 * rows + which, 1), :], (lev, LANES))
        east_corner = jnp.broadcast_to(e_in[pl.ds(2 * rows + which, 1), :], (lev, LANES))
        for k in range(trc):
            c = ref[trc + k]
            far, own = ref[k], mine[trc + k]
            north, south = (own, far) if which == 0 else (far, own)
            here = lane_l == k * lev + sub
            wc = jnp.sum(jnp.where(here, west_corner, 0.0), axis=1, keepdims=True)
            ec = jnp.sum(jnp.where(here, east_corner, 0.0), axis=1, keepdims=True)
            east = jnp.where(lane_l == LANES - 1, ec, pltpu.roll(c, LANES - 1, 1))
            west = jnp.where(lane_l == 0, wc, pltpu.roll(c, 1, 1))
            upper = pltpu.roll(c, lev - 1, 0)
            lower = pltpu.roll(c, 1, 0)
            g = (mid * c + rate[0] * east + rate[1] * west + rate[2] * north + rate[3] * south
                 + rate[4] * upper + rate[5] * lower)
            at = OFF - 1 if which == 0 else OFF + rows
            f1[pl.ds(k * lev * high + at, lev, stride=high), :] = g * mask
    level_of = lane % lev
    for ref, mine, out, side in ((w_in, my_west, gw, 0), (e_in, my_east, ge, 1)):
        cols[pl.ds(OFF, rows), :] = ref[pl.ds(0, rows), :]
        cols[pl.ds(OFF - 1, 1), :] = ref[pl.ds(2 * rows, 1), :]
        cols[pl.ds(OFF + rows, 1), :] = ref[pl.ds(2 * rows + 1, 1), :]
        for r in range(0, rows, 8):
            c = cols[pl.ds(OFF + r, 8), :]
            north, south = cols[pl.ds(OFF + r + 1, 8), :], cols[pl.ds(OFF + r - 1, 8), :]
            far, own = pltpu.roll(c, 64, 1), mine[pl.ds(r, 8), :]
            east, west = (own, far) if side == 0 else (far, own)
            packed = ref[pl.ds(rows + r, 8), :]
            rate = [jnp.take_along_axis(packed, d * lev + level_of, axis=1) for d in range(6)]
            rate[4] = jnp.where(level_of < lev - 1, rate[4], 0.0)
            rate[5] = jnp.where(level_of > 0, rate[5], 0.0)
            mid = 1.0 - rate[0] - rate[1] - rate[2] - rate[3] - rate[4] - rate[5]
            upper, lower = pltpu.roll(c, LANES - 1, 1), pltpu.roll(c, 1, 1)
            out[pl.ds(r, 8), :] = (mid * c + rate[0] * east + rate[1] * west + rate[2] * north + rate[3] * south
                                   + rate[4] * upper + rate[5] * lower)

    def step(load, west_ghost, east_ghost, emit):
        for l in range(lev):
            for r in range(0, rows, 8):
                rate = [tvf[pl.ds((d * lev + l) * rows + r, 8), :] for d in range(6)]
                mid = 1.0 - rate[0] - rate[1] - rate[2] - rate[3]
                if l < lev - 1:
                    mid = mid - rate[4]
                if l > 0:
                    mid = mid - rate[5]
                wg, eg = west_ghost[pl.ds(r, 8), :], east_ghost[pl.ds(r, 8), :]
                for k in range(trc):
                    m = k * lev + l
                    c = load(k, l, r, 0)
                    west = jnp.where(lane == 0, pltpu.roll(wg, (LANES - m) % LANES, 1), pltpu.roll(c, 1, 1))
                    east = jnp.where(lane == LANES - 1, pltpu.roll(eg, LANES - 1 - m, 1), pltpu.roll(c, LANES - 1, 1))
                    v = (mid * c + rate[0] * east + rate[1] * west
                         + rate[2] * load(k, l, r, 1) + rate[3] * load(k, l, r, -1))
                    if l < lev - 1:
                        v = v + rate[4] * load(k, l + 1, r, 0)
                    if l > 0:
                        v = v + rate[5] * load(k, l - 1, r, 0)
                    emit(k, l, r, v)

    def load0(k, l, r, by):
        at = (k * lev + l) * rows + r
        if r + by < 0:
            ghost = bf[pl.ds((trc + k) * lev + l, 8, stride=0), :] * south_mask
            return jnp.where(edge == 0, ghost, pltpu.roll(f0[pl.ds(at, 8), :], 1, 0))
        if r + by + 8 > rows:
            ghost = af[pl.ds((trc + k) * lev + l, 8, stride=0), :] * north_mask
            return jnp.where(edge == 7, ghost, pltpu.roll(f0[pl.ds(at, 8), :], 7, 0))
        return f0[pl.ds(at + by, 8), :]

    def load1(k, l, r, by):
        return f1[pl.ds((k * lev + l) * high + OFF + r + by, 8), :]

    def emit1(k, l, r, v):
        f1[pl.ds((k * lev + l) * high + OFF + r, 8), :] = v

    sums = {}

    def emit2(k, l, r, v):
        lamf[pl.ds((k * lev + l) * rows + r, 8), :] = v
        if l == 0:
            level0[pl.ds(r * trc + k, 8, stride=trc), :] = v
        total = jnp.sum(v, axis=1, keepdims=True)
        old = sums[r] if k else row_sums[pl.ds(r, 8), :]
        sums[r] = jnp.where(lane == l * trc + k, total, old)
        if k == trc - 1:
            row_sums[pl.ds(r, 8), :] = sums[r]

    row_sums[...] = jnp.zeros(row_sums.shape, F32)
    step(load0, w_in, e_in, emit1)
    step(load1, gw, ge, emit2)


def transport(band, bands, field, rates, w_in, e_in, east, west, before, after, up, down, trc, lev, rows):
    high = rows + 2 * OFF
    return call(
        functools.partial(transport_kernel, trc, lev, rows, bands),
        [((trc * lev, rows, LANES), F32), ((rows * trc, LANES), F32), ((rows, LANES), F32)],
        [SMEM] + [VMEM] * 10,
        [
            pltpu.VMEM((trc * lev * high, LANES), F32),
            pltpu.VMEM((high, LANES), F32),
            pltpu.VMEM((rows, LANES), F32),
            pltpu.VMEM((rows, LANES), F32),
        ],
    )(band, field.reshape(trc * lev, rows, LANES), rates.reshape(6 * lev, rows, LANES),
      w_in, e_in, east, west, before, after, up, down)


def tables(region_local, cell_weight, polar_rows, local):
    rows, cols = region_local.shape

    def body(rl, w_ref, p_ref, hot, zc, half, w1, wz):
        eye = iota((rows, rows), 0) == iota((rows, rows), 1)
        flags = jnp.broadcast_to(p_ref[...].astype(F32), (rows, rows))
        hp = 0.5 * jnp.sum(jnp.where(eye, flags, 0.0), axis=1, keepdims=True)
        hp = jnp.broadcast_to(hp, (rows, cols))
        half[...] = hp
        w = w_ref[...]
        w1[...] = w * (1.0 - hp)
        w1z = w * hp
        row_id = iota((rows, cols), 0)
        entry = iota((local, cols), 0)
        for r in range(rows):
            hot[:, pl.ds(r * cols, cols)] = (rl[pl.ds(r, 1), :] == entry).astype(F32).astype(BF16)
            parts = split3(jnp.where(row_id == r, w1z, 0.0))
            for i in range(3):
                wz[pl.ds(i * rows, rows), pl.ds(r * cols, cols)] = parts[i].astype(BF16)
        z = lax.dot_general(wz[...], hot[...], (((1,), (1,)), ((), ())), preferred_element_type=F32)
        zc[...] = z[:rows] + z[rows : 2 * rows] + z[2 * rows :]

    return call(
        body,
        [((local, rows * cols), BF16), ((rows, local), F32), ((rows, cols), F32), ((rows, cols), F32)],
        [VMEM] * 3,
        [pltpu.VMEM((3 * rows, rows * cols), BF16)],
    )(region_local, cell_weight, polar_rows.reshape(1, rows))


def places(tile_regions, own_rows):
    count, local = tile_regions.shape
    regions = own_rows * count
    per = local // count
    owners = LANES // own_rows

    def body(tr, inv):
        lane = iota((8, LANES), 1)

        def block(i, carry):
            t = pl.multiple_of(i * 8, 8)
            for q in range(regions // LANES):
                first = q * owners * per
                src = tr[pl.ds(t, 8), pl.ds(first // LANES * LANES, LANES)]
                start = first % LANES + lane // own_rows * per
                found = jnp.full((8, LANES), -1, jnp.int32)
                for e in range(per):
                    got = jnp.take_along_axis(src, start + e, axis=1)
                    found = jnp.where(got == q * LANES + lane, start + e, found)
                inv[q, pl.ds(t, 8), :] = found
            return carry

        lax.fori_loop(0, count // 8, block, 0)

    return call(body, [((regions // LANES, count, LANES), jnp.int32)], [VMEM])(tile_regions)[0]


def local_sums(level0, w1, hot):
    rows, cols = w1.shape
    trc = level0.shape[0] // rows
    local = hot.shape[0]

    def body(l0, w, hot_ref, out, lhs):
        for r in range(rows):
            s = l0[pl.ds(r * trc, trc), :] * w[pl.ds(r, 1), :]
            hi, mid, lo = split3(s)
            at = pl.ds(r * cols, cols)
            lhs[pl.ds(0, 2 * trc), at] = jnp.concatenate([hi, mid], axis=0).astype(BF16)
            lhs[pl.ds(2 * trc, 2 * trc), at] = jnp.concatenate([lo, jnp.zeros_like(lo)], axis=0).astype(BF16)
        s = lax.dot_general(lhs[...], hot_ref[...], (((1,), (1,)), ((), ())), preferred_element_type=F32)
        out[...] = s[:trc] + s[trc : 2 * trc] + s[2 * trc : 3 * trc]

    return call(body, [((trc, local), F32)], [VMEM] * 3, [pltpu.VMEM((4 * trc, rows * cols), BF16)])(level0, w1, hot)[0]


def regional(parts, s1, zc, trc, devices, columns):
    rows, _ = parts[0].shape
    local = s1.shape[1]

    def body(*refs):
        ins, (s_ref, zc_ref, zonal, out) = refs[: len(parts)], refs[len(parts) :]
        z = ins[0][...]
        for ref in ins[1:]:
            z = z + ref[...]
        z = z / columns
        zonal[...] = z
        s = s_ref[...] + lax.dot_general(
            z[:, :trc], zc_ref[...], (((0,), (0,)), ((), ())), precision=lax.Precision.HIGHEST,
            preferred_element_type=F32)
        for d in range(devices):
            out[d] = s

    return call(body, [((rows, LANES), F32), ((devices, trc, local), F32)], [VMEM] * (len(parts) + 2))(*parts, s1, zc)


def filtered(lam, zonal, half, trc, lev):
    tiles, rows, _ = lam.shape

    def body(l_ref, z_ref, h_ref, out):
        for r in range(0, rows, 8):
            z, h = z_ref[pl.ds(r, 8), :], h_ref[pl.ds(r, 8), :]
            for m in range(tiles):
                i = m % lev * trc + m // lev
                v = l_ref[m, pl.ds(r, 8), :]
                out[m, pl.ds(r, 8), :] = v + h * (jnp.broadcast_to(z[:, i : i + 1], v.shape) - v)

    return call(body, [(lam.shape, F32)], [VMEM] * 3, keep=False)(lam, zonal, half)[0]


def finish(week, sums, inv, cov, base, trc):
    count, _, local = sums.shape
    own_rows, regions = cov.shape
    cols = base.shape[1]
    per = local // count
    owners = LANES // own_rows

    def body(week_ref, s_ref, inv_ref, cov_ref, base_ref, out, fresh):
        def block(q, carry):
            src_at = q * owners * per // LANES * LANES
            src_at = src_at if isinstance(q, int) else pl.multiple_of(src_at, LANES)
            total = [jnp.zeros((trc, LANES), F32) for _ in range(4)]
            for t in range(count):
                idx = inv_ref[q, pl.ds(t, trc, stride=0), :]
                got = jnp.take_along_axis(s_ref[t, :, pl.ds(src_at, LANES)], jnp.maximum(idx, 0), axis=1)
                total[t % 4] = total[t % 4] + jnp.where(idx >= 0, got, 0.0)
            fresh[q] = total[0] + total[1] + (total[2] + total[3])
            return carry

        blocks = regions // LANES
        if blocks <= 16:
            for q in range(blocks):
                block(q, 0)
        else:
            lax.fori_loop(0, blocks, block, 0)
        fresh_rows = jnp.concatenate([fresh[q] for q in range(blocks)], axis=1)
        wide = jnp.concatenate([fresh_rows, jnp.zeros((LANES - trc, regions), F32)], axis=0).astype(BF16)
        added = lax.dot_general(cov_ref[...], wide, (((1,), (1,)), ((), ())), preferred_element_type=F32)
        start = week_ref[0] * trc
        added = pltpu.roll(added, start % LANES, 1)
        for c in range(0, cols, LANES):
            width = min(LANES, cols - c)
            here = jnp.where(start // LANES == c // LANES, added[:, :width], 0.0)
            out[:, pl.ds(c, width)] = base_ref[:, pl.ds(c, width)] + here

    return call(
        body, [((own_rows, cols), F32)], [SMEM] + [VMEM] * 4, [pltpu.VMEM((regions // LANES, trc, LANES), F32)], keep=False
    )(week, sums, inv, cov, base)[0]


def ring(size):
    up = [(i, (i + 1) % size) for i in range(size)]
    return up, [(j, i) for i, j in up]


def partners(devices, bit):
    return [(i, i ^ bit) for i in range(devices)]


def append(parts):
    rows, cols = sum(x.shape[0] for x in parts), parts[0].shape[1]

    def body(*refs):
        at = 0
        for ref in refs[:-1]:
            refs[-1][pl.ds(at, ref.shape[0]), :] = ref[...]
            at += ref.shape[0]

    return call(body, [((rows, cols), parts[0].dtype)], [VMEM] * len(parts))(*parts)[0]


def base_product(tile, mine, theirs, cov, turn):
    own_rows, regions = cov.shape
    cols = mine.shape[1]
    half = len(turn) // 2

    def body(tile_ref, a, b, cov_ref, out, grad):
        for j, flip in enumerate(turn):
            src = a if j < half else b
            at = pl.multiple_of((tile_ref[0] ^ flip) * own_rows, own_rows)
            grad[pl.ds(at, own_rows), :] = src[pl.ds(j % half * own_rows, own_rows), :]
        out[...] = jnp.dot(cov_ref[...], grad[...], preferred_element_type=F32)

    return call(
        body, [((own_rows, cols), F32)], [SMEM] + [VMEM] * 3, [pltpu.VMEM((regions, cols), cov.dtype)]
    )(tile, mine, theirs, cov)[0]


def shards(adjoint, transport_rates, cell_weight, region_local, tile_regions, polar_rows, week_index, grad_in, covariance):
    trc, lev, rows, cols = adjoint.shape
    own_rows, _ = covariance.shape
    lats, lons = lax.axis_size("lat"), lax.axis_size("lon")
    devices = lats * lons
    band = lax.axis_index("lat").astype(jnp.int32).reshape(1)
    tile = band * lons + lax.axis_index("lon").astype(jnp.int32)
    north_to, south_to = ring(lats)
    east_to, west_to = ring(lons)

    lon_bits, bits = lons.bit_length() - 1, devices.bit_length() - 1
    order = list(range(1, lon_bits)) + list(range(lon_bits + 1, bits)) + [0, lon_bits]
    turn = [0]
    for bit in order:
        turn = turn + [j ^ (1 << bit) for j in turn]

    def exchange(i, x):
        return lax.ppermute(x, AXES, partners(devices, 1 << order[i]))

    have = grad_in
    for i in range(len(order) - 1):
        have = append([have, exchange(i, have)])
    theirs = exchange(len(order) - 1, have)

    up, down = border_rows(adjoint, transport_rates)
    before = lax.ppermute(up, "lat", north_to)
    after = lax.ppermute(down, "lat", south_to)
    east, west = border_cols(adjoint, transport_rates)
    east, west = corners(east, west, before, after, band, lats)
    w_in = lax.ppermute(east, "lon", east_to)
    e_in = lax.ppermute(west, "lon", west_to)
    hot, zc, half, w1 = tables(region_local, cell_weight, polar_rows, tile_regions.shape[1])
    inv = places(tile_regions, own_rows)
    lam, level0, row_sums = transport(
        band, lats, adjoint, transport_rates, w_in, e_in, east, west, before, after, up, down, trc, lev, rows)

    if lons <= 4:
        parts = [row_sums] + [lax.ppermute(row_sums, "lon", partners(lons, k)) for k in range(1, lons)]
    else:
        got = lax.all_to_all(
            jnp.broadcast_to(row_sums[None], (lons,) + row_sums.shape), "lon", 0, 0, tiled=True)
        parts = [jnp.sum(got, axis=0)]
    s1 = local_sums(level0, w1, hot)
    zonal, copies = regional(parts, s1, zc, trc, devices, cols * lons)
    sums = lax.all_to_all(copies, AXES, 0, 0, tiled=True)
    adjoint_out = filtered(lam, zonal, half, trc, lev).reshape(adjoint.shape)
    base = base_product(tile, have, theirs, covariance, turn)
    precond = finish(week_index, sums, inv, covariance, base, trc)
    return adjoint_out, precond


def solution(mesh):
    in_specs = (
        P(None, None, "lat", "lon"),
        P(None, None, "lat", "lon"),
        P("lat", "lon"),
        P("lat", "lon"),
        P(),
        P("lat"),
        P(),
        P(("lat", "lon"), None),
        P(("lat", "lon"), None),
    )
    out_specs = (P(None, None, "lat", "lon"), P(("lat", "lon"), None))
    return jax.shard_map(shards, mesh=mesh, in_specs=in_specs, out_specs=out_specs, check_vma=False)
```

```python
import functools
import math

import jax
import jax.numpy as jnp
from jax import lax
from jax.experimental import pallas as pl
from jax.experimental.pallas import tpu as pltpu
from jax.sharding import PartitionSpec as P


AXES = ("lat", "lon")
F32 = jnp.float32
BF16 = jnp.bfloat16
LANES = 128
OFF = 8
VMEM = pl.BlockSpec(memory_space=pltpu.VMEM)
SMEM = pl.BlockSpec(memory_space=pltpu.SMEM)
HBM = pl.BlockSpec(memory_space=pl.ANY)


def iota(shape, dim):
    return lax.broadcasted_iota(jnp.int32, shape, dim)


BIG = 4 << 20


def nbytes(shape, dtype):
    return math.prod(shape) * jnp.dtype(dtype).itemsize


def call(body, outs, in_specs, scratch=(), aliases=None, keep=True):
    def placed(s, d):
        return pltpu.VMEM(s, d) if keep and nbytes(s, d) <= BIG else jax.ShapeDtypeStruct(s, d)

    def apply(*args):
        own = sum(nbytes(x.shape, x.dtype) for x in scratch if getattr(x, "memory_space", None) == pltpu.VMEM)
        own += sum(nbytes(x.shape, x.dtype) for x in args if nbytes(x.shape, x.dtype) > BIG)
        own += sum(nbytes(s, d) for s, d in outs if not keep or nbytes(s, d) > BIG)
        run = pl.pallas_call(
            body,
            out_shape=[placed(s, d) for s, d in outs],
            in_specs=in_specs,
            out_specs=[VMEM] * len(outs),
            scratch_shapes=list(scratch),
            input_output_aliases=aliases or {},
            compiler_params=pltpu.CompilerParams(vmem_limit_bytes=own + (6 << 20)),
        )

        def place(x, spec):
            if spec is HBM:
                return pltpu.with_memory_space_constraint(x, pltpu.HBM)
            if spec is VMEM and nbytes(x.shape, x.dtype) <= BIG:
                return pltpu.with_memory_space_constraint(x, pltpu.VMEM)
            return x

        return run(*(place(x, spec) for x, spec in zip(args, in_specs)))

    return apply


def split3(x):
    hi = x.astype(BF16).astype(F32)
    rest = x - hi
    mid = rest.astype(BF16).astype(F32)
    return hi, mid, rest - mid


def border_rows(field, rates):
    trc, lev, rows, _ = field.shape
    tiles = trc * lev

    def body(f, t, up, down, f_last, f_first, t_last, t_first, sem):
        moves = [
            pltpu.make_async_copy(src.at[:, pl.ds(at, 8), :], dst, sem.at[i])
            for i, (src, at, dst) in enumerate(
                ((f, rows - 8, f_last), (f, 0, f_first), (t, rows - 8, t_last), (t, 0, t_first)))
        ]
        for move in moves:
            move.start()

        def row(ref, group, at):
            return ref.reshape(ref.shape[0] * 8, LANES)[pl.ds(group * lev * 8 + at, lev, stride=8), :]

        moves[0].wait()
        for k in range(trc):
            up[k] = row(f_last, k, 6)
            up[trc + k] = row(f_last, k, 7)
        moves[1].wait()
        for k in range(trc):
            down[k] = row(f_first, k, 1)
            down[trc + k] = row(f_first, k, 0)
        moves[2].wait()
        for d in range(6):
            up[2 * trc + d] = row(t_last, d, 7)
        moves[3].wait()
        for d in range(6):
            down[2 * trc + d] = row(t_first, d, 0)

    out = ((2 * trc + 6, lev, LANES), F32)
    return call(
        body,
        [out, out],
        [HBM, HBM],
        [pltpu.VMEM((n, 8, LANES), F32) for n in (tiles, tiles, 6 * lev, 6 * lev)] + [pltpu.SemaphoreType.DMA((4,))],
    )(field.reshape(tiles, rows, LANES), rates.reshape(6 * lev, rows, LANES))


def border_cols(field, rates):
    trc, lev, rows, _ = field.shape
    tiles = trc * lev

    def body(f, t, east, west):
        lane = iota((8, LANES), 1)
        east[pl.ds(2 * rows, 8), :] = jnp.zeros((8, LANES), F32)
        west[pl.ds(2 * rows, 8), :] = jnp.zeros((8, LANES), F32)
        for c in range(0, rows, 8):
            e = jnp.zeros((8, LANES), F32)
            w = jnp.zeros((8, LANES), F32)
            for m in range(tiles):
                v = f[m, pl.ds(c, 8), :]
                e = jnp.where(lane == m, pltpu.roll(v, (m - 127) % LANES, 1), e)
                e = jnp.where(lane == 64 + m, pltpu.roll(v, (64 + m - 126) % LANES, 1), e)
                w = jnp.where(lane == m, pltpu.roll(v, m % LANES, 1), w)
                w = jnp.where(lane == 64 + m, pltpu.roll(v, (64 + m - 1) % LANES, 1), w)
            east[pl.ds(c, 8), :] = e
            west[pl.ds(c, 8), :] = w
            e = jnp.zeros((8, LANES), F32)
            w = jnp.zeros((8, LANES), F32)
            for j in range(6 * lev):
                v = t[j, pl.ds(c, 8), :]
                e = jnp.where(lane == j, pltpu.roll(v, (j - 127) % LANES, 1), e)
                w = jnp.where(lane == j, pltpu.roll(v, j % LANES, 1), w)
            east[pl.ds(rows + c, 8), :] = e
            west[pl.ds(rows + c, 8), :] = w

    return call(body, [((2 * rows + 8, LANES), F32)] * 2, [VMEM, VMEM])(
        field.reshape(tiles, rows, LANES), rates.reshape(6 * lev, rows, LANES))


def masks(band, bands):
    south = jnp.where(band > 0, 1.0, 0.0).astype(F32)
    north = jnp.where(band < bands - 1, 1.0, 0.0).astype(F32)
    return south, north


def corners(east, west, before, after, band, bands):
    rows = (east.shape[0] - 8) // 2
    lev = before.shape[1]
    trc = (before.shape[0] - 6) // 2

    def body(band_ref, east_in, west_in, b, a, e_ref, w_ref):
        lane, sub = iota((lev, LANES), 1), iota((lev, LANES), 0)
        e_ref[...] = east_in[...]
        w_ref[...] = west_in[...]
        for which, (ref, mask) in enumerate(zip((b, a), masks(band_ref[0], bands))):
            to_e = jnp.zeros((lev, LANES), F32)
            to_w = jnp.zeros((lev, LANES), F32)
            for k in range(trc):
                v = ref[trc + k] * mask
                here = lane == k * lev + sub
                to_e = jnp.where(here, jnp.broadcast_to(v[:, LANES - 1 :], v.shape), to_e)
                to_w = jnp.where(here, jnp.broadcast_to(v[:, :1], v.shape), to_w)
            e_ref[pl.ds(2 * rows + which, 1), :] = jnp.sum(to_e, axis=0, keepdims=True)
            w_ref[pl.ds(2 * rows + which, 1), :] = jnp.sum(to_w, axis=0, keepdims=True)

    return call(body, [(x.shape, F32) for x in (east, west)], [SMEM] + [VMEM] * 4)(
        band, east, west, before, after)


def transport_kernel(trc, lev, rows, bands, band_ref, field, tv, w_in, e_in, my_east, my_west, b, a, my_up, my_down,
                     lam, level0, row_sums, f1, cols, ghost0, ghost1, mids, halves):
    high = rows + 2 * OFF
    lane = iota((8, LANES), 1)
    sub = iota((lev, LANES), 0)
    lane_l = iota((lev, LANES), 1)
    bf, af = (x.reshape((2 * trc + 6) * lev, LANES) for x in (b, a))
    f1_flat = f1.reshape(trc * lev * high, LANES)
    south_mask, north_mask = masks(band_ref[0], bands)
    edge = iota((8, LANES), 0)

    def centre(rate):
        return 1.0 - rate[0] - rate[1] - rate[2] - rate[3] - rate[4] - rate[5]

    for which, (ref, mine, mask) in enumerate(zip((b, a), (my_down, my_up), (south_mask, north_mask))):
        rate = [ref[2 * trc + d] for d in range(6)]
        rate[4] = jnp.where(sub < lev - 1, rate[4], 0.0)
        rate[5] = jnp.where(sub > 0, rate[5], 0.0)
        mid = centre(rate)
        west_corner = jnp.broadcast_to(w_in[pl.ds(2 * rows + which, 1), :], (lev, LANES))
        east_corner = jnp.broadcast_to(e_in[pl.ds(2 * rows + which, 1), :], (lev, LANES))
        for k in range(trc):
            c = ref[trc + k]
            far, own = ref[k], mine[trc + k]
            north, south = (own, far) if which == 0 else (far, own)
            here = lane_l == k * lev + sub
            wc = jnp.sum(jnp.where(here, west_corner, 0.0), axis=1, keepdims=True)
            ec = jnp.sum(jnp.where(here, east_corner, 0.0), axis=1, keepdims=True)
            east = jnp.where(lane_l == LANES - 1, ec, pltpu.roll(c, LANES - 1, 1))
            west = jnp.where(lane_l == 0, wc, pltpu.roll(c, 1, 1))
            upper = pltpu.roll(c, lev - 1, 0)
            lower = pltpu.roll(c, 1, 0)
            g = (mid * c + rate[0] * east + rate[1] * west + rate[2] * north + rate[3] * south
                 + rate[4] * upper + rate[5] * lower)
            at = OFF - 1 if which == 0 else OFF + rows
            f1_flat[pl.ds(k * lev * high + at, lev, stride=high), :] = g * mask
    level_of = lane % lev
    from_west, from_east = lane // 2, (lane + 1) // 2 % 64

    def ghosts(west, east):
        return jnp.where(lane % 2 == 0, jnp.take_along_axis(west, from_west, axis=1),
                         jnp.take_along_axis(east, from_east, axis=1))

    for side, ref in enumerate((w_in, e_in)):
        cols[side, pl.ds(OFF, rows), :] = ref[pl.ds(0, rows), :]
        cols[side, pl.ds(OFF - 1, 1), :] = ref[pl.ds(2 * rows, 1), :]
        cols[side, pl.ds(OFF + rows, 1), :] = ref[pl.ds(2 * rows + 1, 1), :]
    for r in range(0, rows, 8):
        stepped = []
        for side, (ref, mine) in enumerate(((w_in, my_west), (e_in, my_east))):
            c = cols[side, pl.ds(OFF + r, 8), :]
            north, south = cols[side, pl.ds(OFF + r + 1, 8), :], cols[side, pl.ds(OFF + r - 1, 8), :]
            far, own = pltpu.roll(c, 64, 1), mine[pl.ds(r, 8), :]
            east, west = (own, far) if side == 0 else (far, own)
            packed = ref[pl.ds(rows + r, 8), :]
            rate = [jnp.take_along_axis(packed, d * lev + level_of, axis=1) for d in range(6)]
            rate[4] = jnp.where(level_of < lev - 1, rate[4], 0.0)
            rate[5] = jnp.where(level_of > 0, rate[5], 0.0)
            upper, lower = pltpu.roll(c, LANES - 1, 1), pltpu.roll(c, 1, 1)
            stepped.append(centre(rate) * c + rate[0] * east + rate[1] * west + rate[2] * north + rate[3] * south
                           + rate[4] * upper + rate[5] * lower)
        ghost0[pl.ds(r, 8), :] = ghosts(w_in[pl.ds(r, 8), :], e_in[pl.ds(r, 8), :])
        ghost1[pl.ds(r, 8), :] = ghosts(*stepped)
    for l in range(lev):
        for r in range(0, rows, 8):
            rate = [tv[d * lev + l, pl.ds(r, 8), :] for d in range(6)]
            if l == lev - 1:
                rate[4] = jnp.zeros_like(rate[4])
            if l == 0:
                rate[5] = jnp.zeros_like(rate[5])
            mids[l, pl.ds(r, 8), :] = centre(rate)
    row_sums[...] = jnp.zeros(row_sums.shape, F32)

    def step(load, ghost, emit, after):
        def tracer(k, carry):
            for l in range(lev):
                for r in range(0, rows, 8):
                    rate = [tv[d * lev + l, pl.ds(r, 8), :] for d in range(6)]
                    c = load(k, l, r, 0)
                    g = pltpu.roll(ghost[pl.ds(r, 8), :], (LANES - 2 * (k * lev + l)) % LANES, 1)
                    west = jnp.where(lane == 0, g, pltpu.roll(c, 1, 1))
                    east = jnp.where(lane == LANES - 1, g, pltpu.roll(c, LANES - 1, 1))
                    v = (mids[l, pl.ds(r, 8), :] * c + rate[2] * load(k, l, r, 1) + rate[3] * load(k, l, r, -1))
                    if l < lev - 1:
                        v = v + rate[4] * load(k, l + 1, r, 0)
                    if l > 0:
                        v = v + rate[5] * load(k, l - 1, r, 0)
                    emit(k, l, r, v + (rate[0] * east + rate[1] * west))
            after(k)
            return carry

        lax.fori_loop(0, trc, tracer, 0)

    def load0(k, l, r, by):
        m = k * lev + l
        if r + by < 0:
            ghost = bf[pl.ds((trc + k) * lev + l, 8, stride=0), :] * south_mask
            return jnp.where(edge == 0, ghost, pltpu.roll(field[m, pl.ds(0, 8), :], 1, 0))
        if r + by + 8 > rows:
            ghost = af[pl.ds((trc + k) * lev + l, 8, stride=0), :] * north_mask
            return jnp.where(edge == 7, ghost, pltpu.roll(field[m, pl.ds(rows - 8, 8), :], 7, 0))
        return field[m, pl.ds(r + by, 8), :]

    def load1(k, l, r, by):
        return f1[k * lev + l, pl.ds(OFF + r + by, 8), :]

    def emit1(k, l, r, v):
        f1[k * lev + l, pl.ds(OFF + r, 8), :] = v

    def emit2(k, l, r, v):
        lam[k * lev + l, pl.ds(r, 8), :] = v
        if l == 0:
            level0[pl.ds(r * trc + k, 8, stride=trc), :] = v

    def sums(k):
        for l in range(lev):
            for r in range(0, rows, 16):
                v = lam[k * lev + l, pl.ds(r, 16), :]
                hi = v.astype(BF16)
                halves[pl.ds(l * rows + r, 16), pl.ds(0, LANES)] = hi
                halves[pl.ds(l * rows + r, 16), pl.ds(LANES, LANES)] = (v - hi.astype(F32)).astype(BF16)
        total = jnp.dot(halves[...], jnp.ones((2 * LANES, LANES), BF16), preferred_element_type=F32)
        for r in range(0, rows, 8):
            old = row_sums[pl.ds(r, 8), :]
            for l in range(lev):
                old = jnp.where(lane == l * trc + k, total[l * rows + r : l * rows + r + 8], old)
            row_sums[pl.ds(r, 8), :] = old

    step(load0, ghost0, emit1, lambda k: None)
    step(load1, ghost1, emit2, sums)


def transport(band, bands, field, rates, w_in, e_in, east, west, before, after, up, down, trc, lev, rows):
    high = rows + 2 * OFF
    return call(
        functools.partial(transport_kernel, trc, lev, rows, bands),
        [((trc * lev, rows, LANES), F32), ((rows * trc, LANES), F32), ((rows, LANES), F32)],
        [SMEM] + [VMEM] * 10,
        [
            pltpu.VMEM((trc * lev, high, LANES), F32),
            pltpu.VMEM((2, high, LANES), F32),
            pltpu.VMEM((rows, LANES), F32),
            pltpu.VMEM((rows, LANES), F32),
            pltpu.VMEM((lev, rows, LANES), F32),
            pltpu.VMEM((lev * rows, 2 * LANES), BF16),
        ],
    )(band, field.reshape(trc * lev, rows, LANES), rates.reshape(6 * lev, rows, LANES),
      w_in, e_in, east, west, before, after, up, down)


def tables(region_local, cell_weight, polar_rows, local):
    rows, cols = region_local.shape

    def body(rl, w_ref, p_ref, hot, zc, half, w1, wz):
        eye = iota((rows, rows), 0) == iota((rows, rows), 1)
        flags = jnp.broadcast_to(p_ref[...].astype(F32), (rows, rows))
        hp = 0.5 * jnp.sum(jnp.where(eye, flags, 0.0), axis=1, keepdims=True)
        hp = jnp.broadcast_to(hp, (rows, cols))
        half[...] = hp
        w = w_ref[...]
        w1[...] = w * (1.0 - hp)
        w1z = w * hp
        row_id = iota((rows, cols), 0)
        entry = iota((local, cols), 0)
        for r in range(rows):
            hot[:, pl.ds(r * cols, cols)] = (rl[pl.ds(r, 1), :] == entry).astype(F32).astype(BF16)
            parts = split3(jnp.where(row_id == r, w1z, 0.0))
            for i in range(3):
                wz[pl.ds(i * rows, rows), pl.ds(r * cols, cols)] = parts[i].astype(BF16)
        z = lax.dot_general(wz[...], hot[...], (((1,), (1,)), ((), ())), preferred_element_type=F32)
        zc[...] = z[:rows] + z[rows : 2 * rows] + z[2 * rows :]

    return call(
        body,
        [((local, rows * cols), BF16), ((rows, local), F32), ((rows, cols), F32), ((rows, cols), F32)],
        [VMEM] * 3,
        [pltpu.VMEM((3 * rows, rows * cols), BF16)],
    )(region_local, cell_weight, polar_rows.reshape(1, rows))


def places(tile_regions, own_rows):
    count, local = tile_regions.shape
    regions = own_rows * count
    per = local // count
    owners = LANES // own_rows

    def body(tr, inv):
        lane = iota((8, LANES), 1)

        def block(i, carry):
            t = pl.multiple_of(i * 8, 8)
            for q in range(regions // LANES):
                first = q * owners * per
                src = tr[pl.ds(t, 8), pl.ds(first // LANES * LANES, LANES)]
                start = first % LANES + lane // own_rows * per
                found = jnp.full((8, LANES), -1, jnp.int32)
                for e in range(per):
                    got = jnp.take_along_axis(src, start + e, axis=1)
                    found = jnp.where(got == q * LANES + lane, start + e, found)
                inv[q, pl.ds(t, 8), :] = found
            return carry

        lax.fori_loop(0, count // 8, block, 0)

    return call(body, [((regions // LANES, count, LANES), jnp.int32)], [VMEM])(tile_regions)[0]


def local_sums(level0, w1, hot):
    rows, cols = w1.shape
    trc = level0.shape[0] // rows
    local = hot.shape[0]

    def body(l0, w, hot_ref, out, lhs):
        for r in range(rows):
            s = l0[pl.ds(r * trc, trc), :] * w[pl.ds(r, 1), :]
            hi, mid, lo = split3(s)
            at = pl.ds(r * cols, cols)
            lhs[pl.ds(0, 2 * trc), at] = jnp.concatenate([hi, mid], axis=0).astype(BF16)
            lhs[pl.ds(2 * trc, 2 * trc), at] = jnp.concatenate([lo, jnp.zeros_like(lo)], axis=0).astype(BF16)
        s = lax.dot_general(lhs[...], hot_ref[...], (((1,), (1,)), ((), ())), preferred_element_type=F32)
        out[...] = s[:trc] + s[trc : 2 * trc] + s[2 * trc : 3 * trc]

    return call(body, [((trc, local), F32)], [VMEM] * 3, [pltpu.VMEM((4 * trc, rows * cols), BF16)])(level0, w1, hot)[0]


def regional(parts, s1, zc, trc, devices, columns):
    rows, _ = parts[0].shape
    local = s1.shape[1]

    def body(*refs):
        ins, (s_ref, zc_ref, zonal, out) = refs[: len(parts)], refs[len(parts) :]
        z = ins[0][...]
        for ref in ins[1:]:
            z = z + ref[...]
        z = z / columns
        zonal[...] = z
        s = s_ref[...] + lax.dot_general(
            z[:, :trc], zc_ref[...], (((0,), (0,)), ((), ())), precision=lax.Precision.HIGHEST,
            preferred_element_type=F32)
        for d in range(devices):
            out[d] = s

    return call(body, [((rows, LANES), F32), ((devices, trc, local), F32)], [VMEM] * (len(parts) + 2))(*parts, s1, zc)


def filtered(lam, zonal, half, trc, lev):
    tiles, rows, _ = lam.shape

    def body(l_ref, z_ref, h_ref, out):
        for r in range(0, rows, 8):
            z, h = z_ref[pl.ds(r, 8), :], h_ref[pl.ds(r, 8), :]
            for m in range(tiles):
                i = m % lev * trc + m // lev
                v = l_ref[m, pl.ds(r, 8), :]
                out[m, pl.ds(r, 8), :] = v + h * (jnp.broadcast_to(z[:, i : i + 1], v.shape) - v)

    return call(body, [(lam.shape, F32)], [VMEM] * 3, keep=False)(lam, zonal, half)[0]


def finish(week, sums, inv, cov, base, trc):
    count, _, local = sums.shape
    own_rows, regions = cov.shape
    cols = base.shape[1]
    per = local // count
    owners = LANES // own_rows

    def body(week_ref, s_ref, inv_ref, cov_ref, base_ref, out, fresh):
        def block(q, carry):
            src_at = q * owners * per // LANES * LANES
            src_at = src_at if isinstance(q, int) else pl.multiple_of(src_at, LANES)
            total = [jnp.zeros((trc, LANES), F32) for _ in range(4)]
            for t in range(count):
                idx = inv_ref[q, pl.ds(t, trc, stride=0), :]
                got = jnp.take_along_axis(s_ref[t, :, pl.ds(src_at, LANES)], jnp.maximum(idx, 0), axis=1)
                total[t % 4] = total[t % 4] + jnp.where(idx >= 0, got, 0.0)
            fresh[q] = total[0] + total[1] + (total[2] + total[3])
            return carry

        blocks = regions // LANES
        if blocks <= 16:
            for q in range(blocks):
                block(q, 0)
        else:
            lax.fori_loop(0, blocks, block, 0)
        fresh_rows = jnp.concatenate([fresh[q] for q in range(blocks)], axis=1)
        wide = jnp.concatenate([fresh_rows, jnp.zeros((LANES - trc, regions), F32)], axis=0).astype(BF16)
        added = lax.dot_general(cov_ref[...], wide, (((1,), (1,)), ((), ())), preferred_element_type=F32)
        start = week_ref[0] * trc
        added = pltpu.roll(added, start % LANES, 1)
        for c in range(0, cols, LANES):
            width = min(LANES, cols - c)
            here = jnp.where(start // LANES == c // LANES, added[:, :width], 0.0)
            out[:, pl.ds(c, width)] = base_ref[:, pl.ds(c, width)] + here

    return call(
        body, [((own_rows, cols), F32)], [SMEM] + [VMEM] * 4, [pltpu.VMEM((regions // LANES, trc, LANES), F32)], keep=False
    )(week, sums, inv, cov, base)[0]


def ring(size):
    up = [(i, (i + 1) % size) for i in range(size)]
    return up, [(j, i) for i, j in up]


def partners(devices, bit):
    return [(i, i ^ bit) for i in range(devices)]


def append(parts, cols):
    rows = sum(x.shape[0] for x in parts)

    def body(*refs):
        at = 0
        for ref in refs[:-1]:
            here = pl.ds(at, ref.shape[0])
            refs[-1][here, pl.ds(0, ref.shape[1])] = ref[...]
            if cols > ref.shape[1]:
                refs[-1][here, pl.ds(ref.shape[1], cols - ref.shape[1])] = jnp.zeros(
                    (ref.shape[0], cols - ref.shape[1]), ref.dtype)
            at += ref.shape[0]

    return call(body, [((rows, cols), parts[0].dtype)], [VMEM] * len(parts))(*parts)[0]


def base_product(tile, mine, theirs, cov, turn, cols):
    own_rows, regions = cov.shape
    wide = mine.shape[1]
    half = len(turn) // 2

    def body(tile_ref, a, b, cov_ref, out, grad):
        for j, flip in enumerate(turn):
            src = a if j < half else b
            at = pl.multiple_of((tile_ref[0] ^ flip) * own_rows, own_rows)
            grad[pl.ds(at, own_rows), :] = src[pl.ds(j % half * own_rows, own_rows), :]
        out[...] = jnp.dot(cov_ref[...], grad[...], preferred_element_type=F32)[:, :cols]

    return call(
        body, [((own_rows, cols), F32)], [SMEM] + [VMEM] * 3, [pltpu.VMEM((regions, wide), cov.dtype)]
    )(tile, mine, theirs, cov)[0]


def shards(adjoint, transport_rates, cell_weight, region_local, tile_regions, polar_rows, week_index, grad_in, covariance):
    trc, lev, rows, cols = adjoint.shape
    own_rows, _ = covariance.shape
    lats, lons = lax.axis_size("lat"), lax.axis_size("lon")
    devices = lats * lons
    band = lax.axis_index("lat").astype(jnp.int32).reshape(1)
    tile = band * lons + lax.axis_index("lon").astype(jnp.int32)
    north_to, south_to = ring(lats)
    east_to, west_to = ring(lons)

    lon_bits, bits = lons.bit_length() - 1, devices.bit_length() - 1
    far = list(range(lon_bits + 1, bits))
    order = list(range(lon_bits - 1, 0, -1)) + far[:1] + [0] + far[1:] + [lon_bits]
    turn = [0]
    for bit in order:
        turn = turn + [j ^ (1 << bit) for j in turn]

    def exchange(i, x):
        return lax.ppermute(x, AXES, partners(devices, 1 << order[i]))

    have = grad_in
    for i in range(len(order) - 1):
        wide = pl.cdiv(have.shape[1], LANES) * LANES if i == len(order) - 2 else have.shape[1]
        have = append([have, exchange(i, have)], wide)
    theirs = exchange(len(order) - 1, have)

    up, down = border_rows(adjoint, transport_rates)
    before = lax.ppermute(up, "lat", north_to)
    after = lax.ppermute(down, "lat", south_to)
    east, west = border_cols(adjoint, transport_rates)
    east, west = corners(east, west, before, after, band, lats)
    w_in = lax.ppermute(east, "lon", east_to)
    e_in = lax.ppermute(west, "lon", west_to)
    hot, zc, half, w1 = tables(region_local, cell_weight, polar_rows, tile_regions.shape[1])
    inv = places(tile_regions, own_rows)
    lam, level0, row_sums = transport(
        band, lats, adjoint, transport_rates, w_in, e_in, east, west, before, after, up, down, trc, lev, rows)

    if lons <= 4:
        parts = [row_sums] + [lax.ppermute(row_sums, "lon", partners(lons, k)) for k in range(1, lons)]
    else:
        got = lax.all_to_all(
            jnp.broadcast_to(row_sums[None], (lons,) + row_sums.shape), "lon", 0, 0, tiled=True)
        parts = [jnp.sum(got, axis=0)]
    s1 = local_sums(level0, w1, hot)
    zonal, copies = regional(parts, s1, zc, trc, devices, cols * lons)
    sums = lax.all_to_all(copies, AXES, 0, 0, tiled=True)
    adjoint_out = filtered(lam, zonal, half, trc, lev).reshape(adjoint.shape)
    base = base_product(tile, have, theirs, covariance, turn, grad_in.shape[1])
    precond = finish(week_index, sums, inv, covariance, base, trc)
    return adjoint_out, precond


def solution(mesh):
    in_specs = (
        P(None, None, "lat", "lon"),
        P(None, None, "lat", "lon"),
        P("lat", "lon"),
        P("lat", "lon"),
        P(),
        P("lat"),
        P(),
        P(("lat", "lon"), None),
        P(("lat", "lon"), None),
    )
    out_specs = (P(None, None, "lat", "lon"), P(("lat", "lon"), None))
    return jax.shard_map(shards, mesh=mesh, in_specs=in_specs, out_specs=out_specs, check_vma=False)
```

```python
import functools
import math

import jax
import jax.numpy as jnp
from jax import lax
from jax.experimental import pallas as pl
from jax.experimental.pallas import tpu as pltpu
from jax.sharding import PartitionSpec as P


AXES = ("lat", "lon")
F32 = jnp.float32
BF16 = jnp.bfloat16
LANES = 128
OFF = 8
VMEM = pl.BlockSpec(memory_space=pltpu.VMEM)
SMEM = pl.BlockSpec(memory_space=pltpu.SMEM)
HBM = pl.BlockSpec(memory_space=pl.ANY)


def iota(shape, dim):
    return lax.broadcasted_iota(jnp.int32, shape, dim)


BIG = 4 << 20


def nbytes(shape, dtype):
    return math.prod(shape) * jnp.dtype(dtype).itemsize


def call(body, outs, in_specs, scratch=(), aliases=None, keep=True):
    def placed(s, d):
        return pltpu.VMEM(s, d) if keep and nbytes(s, d) <= BIG else jax.ShapeDtypeStruct(s, d)

    def apply(*args):
        own = sum(nbytes(x.shape, x.dtype) for x in scratch if getattr(x, "memory_space", None) == pltpu.VMEM)
        own += sum(nbytes(x.shape, x.dtype) for x in args if nbytes(x.shape, x.dtype) > BIG)
        own += sum(nbytes(s, d) for s, d in outs if not keep or nbytes(s, d) > BIG)
        run = pl.pallas_call(
            body,
            out_shape=[placed(s, d) for s, d in outs],
            in_specs=in_specs,
            out_specs=[VMEM] * len(outs),
            scratch_shapes=list(scratch),
            input_output_aliases=aliases or {},
            compiler_params=pltpu.CompilerParams(vmem_limit_bytes=own + (6 << 20)),
        )

        def place(x, spec):
            if spec is HBM:
                return pltpu.with_memory_space_constraint(x, pltpu.HBM)
            if spec is VMEM and nbytes(x.shape, x.dtype) <= BIG:
                return pltpu.with_memory_space_constraint(x, pltpu.VMEM)
            return x

        return run(*(place(x, spec) for x, spec in zip(args, in_specs)))

    return apply


def split3(x):
    hi = x.astype(BF16).astype(F32)
    rest = x - hi
    mid = rest.astype(BF16).astype(F32)
    return hi, mid, rest - mid


def border_rows(field, rates):
    trc, lev, rows, _ = field.shape
    tiles = trc * lev

    def body(f, t, up, down, f_last, f_first, t_last, t_first, sem):
        moves = [
            pltpu.make_async_copy(src.at[:, pl.ds(at, 8), :], dst, sem.at[i])
            for i, (src, at, dst) in enumerate(
                ((f, rows - 8, f_last), (f, 0, f_first), (t, rows - 8, t_last), (t, 0, t_first)))
        ]
        for move in moves:
            move.start()

        def row(ref, group, at):
            return ref.reshape(ref.shape[0] * 8, LANES)[pl.ds(group * lev * 8 + at, lev, stride=8), :]

        moves[0].wait()
        for k in range(trc):
            up[k] = row(f_last, k, 6)
            up[trc + k] = row(f_last, k, 7)
        moves[1].wait()
        for k in range(trc):
            down[k] = row(f_first, k, 1)
            down[trc + k] = row(f_first, k, 0)
        moves[2].wait()
        for d in range(6):
            up[2 * trc + d] = row(t_last, d, 7)
        moves[3].wait()
        for d in range(6):
            down[2 * trc + d] = row(t_first, d, 0)

    out = ((2 * trc + 6, lev, LANES), F32)
    return call(
        body,
        [out, out],
        [HBM, HBM],
        [pltpu.VMEM((n, 8, LANES), F32) for n in (tiles, tiles, 6 * lev, 6 * lev)] + [pltpu.SemaphoreType.DMA((4,))],
    )(field.reshape(tiles, rows, LANES), rates.reshape(6 * lev, rows, LANES))


def border_cols(field, rates):
    trc, lev, rows, _ = field.shape
    tiles = trc * lev

    def body(f, t, east, west):
        lane = iota((8, LANES), 1)
        east[pl.ds(2 * rows, 8), :] = jnp.zeros((8, LANES), F32)
        west[pl.ds(2 * rows, 8), :] = jnp.zeros((8, LANES), F32)
        for c in range(0, rows, 8):
            e = jnp.zeros((8, LANES), F32)
            w = jnp.zeros((8, LANES), F32)
            for m in range(tiles):
                v = f[m, pl.ds(c, 8), :]
                e = jnp.where(lane == m, pltpu.roll(v, (m - 127) % LANES, 1), e)
                e = jnp.where(lane == 64 + m, pltpu.roll(v, (64 + m - 126) % LANES, 1), e)
                w = jnp.where(lane == m, pltpu.roll(v, m % LANES, 1), w)
                w = jnp.where(lane == 64 + m, pltpu.roll(v, (64 + m - 1) % LANES, 1), w)
            east[pl.ds(c, 8), :] = e
            west[pl.ds(c, 8), :] = w
            e = jnp.zeros((8, LANES), F32)
            w = jnp.zeros((8, LANES), F32)
            for j in range(6 * lev):
                v = t[j, pl.ds(c, 8), :]
                e = jnp.where(lane == j, pltpu.roll(v, (j - 127) % LANES, 1), e)
                w = jnp.where(lane == j, pltpu.roll(v, j % LANES, 1), w)
            east[pl.ds(rows + c, 8), :] = e
            west[pl.ds(rows + c, 8), :] = w

    return call(body, [((2 * rows + 8, LANES), F32)] * 2, [VMEM, VMEM])(
        field.reshape(tiles, rows, LANES), rates.reshape(6 * lev, rows, LANES))


def masks(band, bands):
    south = jnp.where(band > 0, 1.0, 0.0).astype(F32)
    north = jnp.where(band < bands - 1, 1.0, 0.0).astype(F32)
    return south, north


def corners(east, west, before, after, bands):
    rows = (east.shape[0] - 8) // 2
    lev = before.shape[1]
    trc = (before.shape[0] - 6) // 2

    def body(east_in, west_in, b, a, e_ref, w_ref):
        lane, sub = iota((lev, LANES), 1), iota((lev, LANES), 0)
        e_ref[...] = east_in[...]
        w_ref[...] = west_in[...]
        for which, (ref, mask) in enumerate(zip((b, a), masks(lax.axis_index("lat"), bands))):
            to_e = jnp.zeros((lev, LANES), F32)
            to_w = jnp.zeros((lev, LANES), F32)
            for k in range(trc):
                v = ref[trc + k] * mask
                here = lane == k * lev + sub
                to_e = jnp.where(here, jnp.broadcast_to(v[:, LANES - 1 :], v.shape), to_e)
                to_w = jnp.where(here, jnp.broadcast_to(v[:, :1], v.shape), to_w)
            e_ref[pl.ds(2 * rows + which, 1), :] = jnp.sum(to_e, axis=0, keepdims=True)
            w_ref[pl.ds(2 * rows + which, 1), :] = jnp.sum(to_w, axis=0, keepdims=True)

    return call(body, [(x.shape, F32) for x in (east, west)], [VMEM] * 4)(
        east, west, before, after)


def transport_kernel(trc, lev, rows, bands, field, tv, w_in, e_in, my_east, my_west, b, a, my_up, my_down,
                     lam, level0, row_sums, f1, cols, ghost0, ghost1, mids, halves):
    high = rows + 2 * OFF
    lane = iota((8, LANES), 1)
    sub = iota((lev, LANES), 0)
    lane_l = iota((lev, LANES), 1)
    bf, af = (x.reshape((2 * trc + 6) * lev, LANES) for x in (b, a))
    f1_flat = f1.reshape(trc * lev * high, LANES)
    south_mask, north_mask = masks(lax.axis_index("lat"), bands)
    edge = iota((8, LANES), 0)

    def centre(rate):
        return 1.0 - rate[0] - rate[1] - rate[2] - rate[3] - rate[4] - rate[5]

    for which, (ref, mine, mask) in enumerate(zip((b, a), (my_down, my_up), (south_mask, north_mask))):
        rate = [ref[2 * trc + d] for d in range(6)]
        rate[4] = jnp.where(sub < lev - 1, rate[4], 0.0)
        rate[5] = jnp.where(sub > 0, rate[5], 0.0)
        mid = centre(rate)
        west_corner = jnp.broadcast_to(w_in[pl.ds(2 * rows + which, 1), :], (lev, LANES))
        east_corner = jnp.broadcast_to(e_in[pl.ds(2 * rows + which, 1), :], (lev, LANES))
        for k in range(trc):
            c = ref[trc + k]
            far, own = ref[k], mine[trc + k]
            north, south = (own, far) if which == 0 else (far, own)
            here = lane_l == k * lev + sub
            wc = jnp.sum(jnp.where(here, west_corner, 0.0), axis=1, keepdims=True)
            ec = jnp.sum(jnp.where(here, east_corner, 0.0), axis=1, keepdims=True)
            east = jnp.where(lane_l == LANES - 1, ec, pltpu.roll(c, LANES - 1, 1))
            west = jnp.where(lane_l == 0, wc, pltpu.roll(c, 1, 1))
            upper = pltpu.roll(c, lev - 1, 0)
            lower = pltpu.roll(c, 1, 0)
            g = (mid * c + rate[0] * east + rate[1] * west + rate[2] * north + rate[3] * south
                 + rate[4] * upper + rate[5] * lower)
            at = OFF - 1 if which == 0 else OFF + rows
            f1_flat[pl.ds(k * lev * high + at, lev, stride=high), :] = g * mask
    level_of = lane % lev
    from_west, from_east = lane // 2, (lane + 1) // 2 % 64

    def ghosts(west, east):
        return jnp.where(lane % 2 == 0, jnp.take_along_axis(west, from_west, axis=1),
                         jnp.take_along_axis(east, from_east, axis=1))

    for side, ref in enumerate((w_in, e_in)):
        cols[side, pl.ds(OFF, rows), :] = ref[pl.ds(0, rows), :]
        cols[side, pl.ds(OFF - 1, 1), :] = ref[pl.ds(2 * rows, 1), :]
        cols[side, pl.ds(OFF + rows, 1), :] = ref[pl.ds(2 * rows + 1, 1), :]
    for r in range(0, rows, 8):
        stepped = []
        for side, (ref, mine) in enumerate(((w_in, my_west), (e_in, my_east))):
            c = cols[side, pl.ds(OFF + r, 8), :]
            north, south = cols[side, pl.ds(OFF + r + 1, 8), :], cols[side, pl.ds(OFF + r - 1, 8), :]
            far, own = pltpu.roll(c, 64, 1), mine[pl.ds(r, 8), :]
            east, west = (own, far) if side == 0 else (far, own)
            packed = ref[pl.ds(rows + r, 8), :]
            rate = [jnp.take_along_axis(packed, d * lev + level_of, axis=1) for d in range(6)]
            rate[4] = jnp.where(level_of < lev - 1, rate[4], 0.0)
            rate[5] = jnp.where(level_of > 0, rate[5], 0.0)
            upper, lower = pltpu.roll(c, LANES - 1, 1), pltpu.roll(c, 1, 1)
            stepped.append(centre(rate) * c + rate[0] * east + rate[1] * west + rate[2] * north + rate[3] * south
                           + rate[4] * upper + rate[5] * lower)
        ghost0[pl.ds(r, 8), :] = ghosts(w_in[pl.ds(r, 8), :], e_in[pl.ds(r, 8), :])
        ghost1[pl.ds(r, 8), :] = ghosts(*stepped)
    for l in range(lev):
        for r in range(0, rows, 8):
            rate = [tv[d * lev + l, pl.ds(r, 8), :] for d in range(6)]
            if l == lev - 1:
                rate[4] = jnp.zeros_like(rate[4])
            if l == 0:
                rate[5] = jnp.zeros_like(rate[5])
            mids[l, pl.ds(r, 8), :] = centre(rate)

    def step(load, ghost, emit, after):
        def tracer(k, carry):
            for l in range(lev):
                for r in range(0, rows, 8):
                    rate = [tv[d * lev + l, pl.ds(r, 8), :] for d in range(6)]
                    c = load(k, l, r, 0)
                    g = pltpu.roll(ghost[pl.ds(r, 8), :], (LANES - 2 * (k * lev + l)) % LANES, 1)
                    west = jnp.where(lane == 0, g, pltpu.roll(c, 1, 1))
                    east = jnp.where(lane == LANES - 1, g, pltpu.roll(c, LANES - 1, 1))
                    v = (mids[l, pl.ds(r, 8), :] * c + rate[2] * load(k, l, r, 1) + rate[3] * load(k, l, r, -1))
                    if l < lev - 1:
                        v = v + rate[4] * load(k, l + 1, r, 0)
                    if l > 0:
                        v = v + rate[5] * load(k, l - 1, r, 0)
                    emit(k, l, r, v + (rate[0] * east + rate[1] * west))
            after(k)
            return carry

        lax.fori_loop(0, trc, tracer, 0)

    def load0(k, l, r, by):
        m = k * lev + l
        if r + by < 0:
            ghost = bf[pl.ds((trc + k) * lev + l, 8, stride=0), :] * south_mask
            return jnp.where(edge == 0, ghost, pltpu.roll(field[m, pl.ds(0, 8), :], 1, 0))
        if r + by + 8 > rows:
            ghost = af[pl.ds((trc + k) * lev + l, 8, stride=0), :] * north_mask
            return jnp.where(edge == 7, ghost, pltpu.roll(field[m, pl.ds(rows - 8, 8), :], 7, 0))
        return field[m, pl.ds(r + by, 8), :]

    def load1(k, l, r, by):
        return f1[k * lev + l, pl.ds(OFF + r + by, 8), :]

    def emit1(k, l, r, v):
        f1[k * lev + l, pl.ds(OFF + r, 8), :] = v

    def emit2(k, l, r, v):
        lam[k * lev + l, pl.ds(r, 8), :] = v
        if l == 0:
            level0[pl.ds(r * trc + k, 8, stride=trc), :] = v

    def halve(k):
        for l in range(lev):
            for r in range(0, rows, 16):
                v = lam[k * lev + l, pl.ds(r, 16), :]
                hi = v.astype(BF16)
                halves[k, pl.ds(l * rows + r, 16), pl.ds(0, LANES)] = hi
                halves[k, pl.ds(l * rows + r, 16), pl.ds(LANES, LANES)] = (v - hi.astype(F32)).astype(BF16)

    step(load0, ghost0, emit1, lambda k: None)
    step(load1, ghost1, emit2, halve)
    total = [jnp.zeros((8, LANES), F32) for _ in range(0, rows, 8)]
    ones = jnp.ones((2 * LANES, LANES), BF16)
    for k in range(trc):
        sums = jnp.dot(halves[k], ones, preferred_element_type=F32)
        for l in range(lev):
            for i in range(rows // 8):
                at = l * rows + 8 * i
                total[i] = jnp.where(lane == l * trc + k, sums[at : at + 8], total[i])
    for i in range(rows // 8):
        row_sums[pl.ds(8 * i, 8), :] = total[i]


def transport(bands, field, rates, w_in, e_in, east, west, before, after, up, down, trc, lev, rows):
    high = rows + 2 * OFF
    return call(
        functools.partial(transport_kernel, trc, lev, rows, bands),
        [((trc * lev, rows, LANES), F32), ((rows * trc, LANES), F32), ((rows, LANES), F32)],
        [VMEM] * 10,
        [
            pltpu.VMEM((trc * lev, high, LANES), F32),
            pltpu.VMEM((2, high, LANES), F32),
            pltpu.VMEM((rows, LANES), F32),
            pltpu.VMEM((rows, LANES), F32),
            pltpu.VMEM((lev, rows, LANES), F32),
            pltpu.VMEM((trc, lev * rows, 2 * LANES), BF16),
        ],
    )(field.reshape(trc * lev, rows, LANES), rates.reshape(6 * lev, rows, LANES),
      w_in, e_in, east, west, before, after, up, down)


def numbered(row, each, blocks):
    return (row & (blocks - 1)) * each + (row >> (blocks.bit_length() - 1))


def tables(region_local, cell_weight, polar_rows, local, blocks):
    rows, cols = region_local.shape

    def body(rl, w_ref, p_ref, hot, zc, half, w1, wz):
        eye = iota((rows, rows), 0) == iota((rows, rows), 1)
        flags = jnp.broadcast_to(p_ref[...].astype(F32), (rows, rows))
        hp = 0.5 * jnp.sum(jnp.where(eye, flags, 0.0), axis=1, keepdims=True)
        hp = jnp.broadcast_to(hp, (rows, cols))
        half[...] = hp
        w = w_ref[...]
        w1[...] = w * (1.0 - hp)
        w1z = w * hp
        row_id = iota((rows, cols), 0)
        entry = numbered(iota((local, cols), 0), local // blocks, blocks)
        for r in range(rows):
            hot[:, pl.ds(r * cols, cols)] = (rl[pl.ds(r, 1), :] == entry).astype(F32).astype(BF16)
            parts = split3(jnp.where(row_id == r, w1z, 0.0))
            for i in range(3):
                wz[pl.ds(i * rows, rows), pl.ds(r * cols, cols)] = parts[i].astype(BF16)
        z = lax.dot_general(wz[...], hot[...], (((1,), (1,)), ((), ())), preferred_element_type=F32)
        z = z[:rows] + z[rows : 2 * rows] + z[2 * rows :]
        hi, mid, lo = split3(jnp.concatenate([z, jnp.zeros((LANES - rows, local), F32)], axis=0))
        for i, piece in enumerate((hi, mid, lo)):
            turned = jnp.transpose(piece)[:, :rows].astype(BF16)
            for at in ((0, 3, 5), (1, 4), (2,))[i]:
                zc[:, pl.ds(at * rows, rows)] = turned

    return call(
        body,
        [((local, rows * cols), BF16), ((local, 6 * rows), BF16), ((rows, cols), F32), ((rows, cols), F32)],
        [VMEM] * 3,
        [pltpu.VMEM((3 * rows, rows * cols), BF16)],
    )(region_local, cell_weight, polar_rows.reshape(1, rows))


def places(tile_regions, own_rows):
    count, local = tile_regions.shape
    regions = own_rows * count
    blocks = regions // LANES
    each = local // blocks
    width = count * each
    group = LANES // each

    def body(tr, out):
        lane, sub = iota((group, LANES), 1), iota((group, LANES), 0)
        region = iota((LANES, LANES), 0)

        def block(q, carry):
            first = q * each
            src_at = pl.multiple_of(first // LANES * LANES, LANES)
            from_lane = first % LANES + lane % each
            for g in range(width // LANES):
                src = tr[pl.ds(g * group, group), pl.ds(src_at, LANES)]
                got = jnp.take_along_axis(src, from_lane, axis=1)
                row = jnp.sum(jnp.where(lane // each == sub, got, 0), axis=0, keepdims=True)
                out[pl.ds(pl.multiple_of(q * LANES, LANES), LANES), pl.ds(g * LANES, LANES)] = (
                    (row == q * LANES + region).astype(F32).astype(BF16))
            return carry

        lax.fori_loop(0, blocks, block, 0)

    return call(body, [((regions, width), BF16)], [VMEM])(tile_regions)[0]


def local_sums(level0, w1, hot):
    rows, cols = w1.shape
    trc = level0.shape[0] // rows
    local = hot.shape[0]

    def body(l0, w, hot_ref, out, lhs):
        for r in range(rows):
            s = l0[pl.ds(r * trc, trc), :] * w[pl.ds(r, 1), :]
            hi, mid, lo = split3(s)
            at = pl.ds(r * cols, cols)
            lhs[pl.ds(0, 2 * trc), at] = jnp.concatenate([hi, mid], axis=0).astype(BF16)
            lhs[pl.ds(2 * trc, 2 * trc), at] = jnp.concatenate([lo, jnp.zeros_like(lo)], axis=0).astype(BF16)
        s = lax.dot_general(lhs[...], hot_ref[...], (((1,), (1,)), ((), ())), preferred_element_type=F32)
        s = s[:trc] + s[trc : 2 * trc] + s[2 * trc : 3 * trc]
        out[...] = jnp.transpose(jnp.concatenate([s, jnp.zeros((LANES - trc, local), F32)], axis=0))

    return call(
        body, [((local, LANES), F32)], [VMEM] * 3, [pltpu.VMEM((4 * trc, rows * cols), BF16)]
    )(level0, w1, hot)[0]


def regional(parts, s1, zc, trc, devices, columns, blocks):
    rows, _ = parts[0].shape
    local = s1.shape[0]
    each, width = local // blocks, blocks * trc

    def body(*refs):
        ins, (s_ref, zc_ref, zonal, out, mixed) = refs[: len(parts)], refs[len(parts) :]
        z = ins[0][...]
        for ref in ins[1:]:
            z = z + ref[...]
        z = z / columns
        zonal[...] = z
        hi, mid, lo = split3(z)
        pieces = jnp.concatenate([x.astype(BF16) for x in (hi, hi, hi, mid, mid, lo)], axis=0)
        more = jnp.dot(zc_ref[...], pieces, preferred_element_type=F32)
        mixed[...] = s_ref[...] + jnp.where(iota((local, LANES), 1) < trc, more, 0.0)
        for c in range(0, width, LANES):
            total = jnp.zeros((each, LANES), F32)
            for q in range(c // trc, (c + LANES) // trc):
                total = total + pltpu.roll(mixed[pl.ds(q, each, stride=blocks), :], q * trc % LANES, 1)
            for d in range(devices):
                out[d, :, pl.ds(c, LANES)] = total

    return call(
        body, [((rows, LANES), F32), ((devices, each, width), F32)], [VMEM] * (len(parts) + 2),
        [pltpu.VMEM((local, LANES), F32)]
    )(*parts, s1, zc)


def filtered(lam, zonal, half, trc, lev):
    tiles, rows, _ = lam.shape

    def body(l_ref, z_ref, h_ref, out):
        for r in range(0, rows, 8):
            z, h = z_ref[pl.ds(r, 8), :], h_ref[pl.ds(r, 8), :]
            for m in range(tiles):
                i = m % lev * trc + m // lev
                v = l_ref[m, pl.ds(r, 8), :]
                out[m, pl.ds(r, 8), :] = v + h * (jnp.broadcast_to(z[:, i : i + 1], v.shape) - v)

    return call(body, [(lam.shape, F32)], [VMEM] * 3, keep=False)(lam, zonal, half)[0]


def finish(week, sums, hot, cov, base, trc):
    own_rows, _ = cov.shape
    cols = base.shape[1]
    width = sums.shape[1]
    span = LANES // trc * LANES

    def body(week_ref, s_ref, hot_ref, cov_ref, base_ref, out):
        added = jnp.zeros((own_rows, LANES), F32)
        for c in range(0, width, LANES):
            parts = [x.astype(BF16) for x in split3(jnp.transpose(s_ref[:, pl.ds(c, LANES)]))]
            fresh = []
            for q in range(0, LANES // trc, 2):
                rows = slice(q * trc, (q + 2) * trc)
                both = lax.dot_general(
                    jnp.concatenate([x[rows] for x in parts], axis=0),
                    hot_ref[pl.ds((c // trc + q) * LANES, 2 * LANES), :],
                    (((1,), (1,)), ((), ())), preferred_element_type=F32)
                both = both[: 2 * trc] + both[2 * trc : 4 * trc] + both[4 * trc :]
                fresh += [both[:trc, :LANES], both[trc:, LANES:]]
            fresh = jnp.concatenate(fresh, axis=1)
            fresh = jnp.concatenate([fresh] * (LANES // trc), axis=0).astype(BF16)
            added = added + lax.dot_general(
                cov_ref[:, pl.ds(c // trc * LANES, span)], fresh, (((1,), (1,)), ((), ())),
                preferred_element_type=F32)
        for c in range(0, cols, LANES):
            w = min(LANES, cols - c)
            here = (c + iota((own_rows, LANES), 1)) // trc == week_ref[0]
            out[:, pl.ds(c, w)] = base_ref[:, pl.ds(c, w)] + jnp.where(here, added, 0.0)[:, :w]

    return call(body, [((own_rows, cols), F32)], [SMEM] + [VMEM] * 4, keep=False)(
        week, sums, hot, cov, base)[0]


def ring(size):
    up = [(i, (i + 1) % size) for i in range(size)]
    return up, [(j, i) for i, j in up]


def partners(devices, bit):
    return [(i, i ^ bit) for i in range(devices)]


def append(parts, cols):
    rows = sum(x.shape[0] for x in parts)

    def body(*refs):
        at = 0
        for ref in refs[:-1]:
            here = pl.ds(at, ref.shape[0])
            refs[-1][here, pl.ds(0, ref.shape[1])] = ref[...]
            if cols > ref.shape[1]:
                refs[-1][here, pl.ds(ref.shape[1], cols - ref.shape[1])] = jnp.zeros(
                    (ref.shape[0], cols - ref.shape[1]), ref.dtype)
            at += ref.shape[0]

    return call(body, [((rows, cols), parts[0].dtype)], [VMEM] * len(parts))(*parts)[0]


def base_product(mine, theirs, cov, turn, cols):
    own_rows, regions = cov.shape
    wide = mine.shape[1]
    half = len(turn) // 2

    def body(a, b, cov_ref, out, grad):
        tile = lax.axis_index("lat") * lax.axis_size("lon") + lax.axis_index("lon")
        for j, flip in enumerate(turn):
            src = a if j < half else b
            at = pl.multiple_of((tile ^ flip) * own_rows, own_rows)
            grad[pl.ds(at, own_rows), :] = src[pl.ds(j % half * own_rows, own_rows), :]
        out[...] = jnp.dot(cov_ref[...], grad[...], preferred_element_type=F32)[:, :cols]

    return call(
        body, [((own_rows, cols), F32)], [VMEM] * 3, [pltpu.VMEM((regions, wide), cov.dtype)]
    )(mine, theirs, cov)[0]


def shards(adjoint, transport_rates, cell_weight, region_local, tile_regions, polar_rows, week_index, grad_in, covariance):
    trc, lev, rows, cols = adjoint.shape
    own_rows, regions = covariance.shape
    lats, lons = lax.axis_size("lat"), lax.axis_size("lon")
    devices = lats * lons
    north_to, south_to = ring(lats)
    east_to, west_to = ring(lons)

    lon_bits, bits = lons.bit_length() - 1, devices.bit_length() - 1
    far = list(range(lon_bits + 1, bits))
    order = list(range(lon_bits - 1, 0, -1)) + far[:1] + [0] + far[1:] + [lon_bits]
    turn = [0]
    for bit in order:
        turn = turn + [j ^ (1 << bit) for j in turn]

    def exchange(i, x):
        return lax.ppermute(x, AXES, partners(devices, 1 << order[i]))

    have = grad_in
    for i in range(len(order) - 1):
        wide = pl.cdiv(have.shape[1], LANES) * LANES if i == len(order) - 2 else have.shape[1]
        have = append([have, exchange(i, have)], wide)
    theirs = exchange(len(order) - 1, have)

    up, down = border_rows(adjoint, transport_rates)
    before = lax.ppermute(up, "lat", north_to)
    after = lax.ppermute(down, "lat", south_to)
    east, west = border_cols(adjoint, transport_rates)
    east, west = corners(east, west, before, after, lats)
    w_in = lax.ppermute(east, "lon", east_to)
    e_in = lax.ppermute(west, "lon", west_to)
    blocks = regions // LANES
    hot, zc, half, w1 = tables(region_local, cell_weight, polar_rows, tile_regions.shape[1], blocks)
    where = places(tile_regions, own_rows)
    lam, level0, row_sums = transport(
        lats, adjoint, transport_rates, w_in, e_in, east, west, before, after, up, down, trc, lev, rows)

    if lons <= 4:
        parts = [row_sums] + [lax.ppermute(row_sums, "lon", partners(lons, k)) for k in range(1, lons)]
    else:
        got = lax.all_to_all(
            jnp.broadcast_to(row_sums[None], (lons,) + row_sums.shape), "lon", 0, 0, tiled=True)
        parts = [jnp.sum(got, axis=0)]
    s1 = local_sums(level0, w1, hot)
    zonal, copies = regional(parts, s1, zc, trc, devices, cols * lons, blocks)
    sums = lax.all_to_all(copies, AXES, 0, 0, tiled=True)
    sums = sums.reshape(-1, sums.shape[2])
    adjoint_out = filtered(lam, zonal, half, trc, lev).reshape(adjoint.shape)
    base = base_product(have, theirs, covariance, turn, grad_in.shape[1])
    precond = finish(week_index, sums, where, covariance, base, trc)
    return adjoint_out, precond


def solution(mesh):
    in_specs = (
        P(None, None, "lat", "lon"),
        P(None, None, "lat", "lon"),
        P("lat", "lon"),
        P("lat", "lon"),
        P(),
        P("lat"),
        P(),
        P(("lat", "lon"), None),
        P(("lat", "lon"), None),
    )
    out_specs = (P(None, None, "lat", "lon"), P(("lat", "lon"), None))
    return jax.shard_map(shards, mesh=mesh, in_specs=in_specs, out_specs=out_specs, check_vma=False)
```

```python
import functools
import math

import jax
import jax.numpy as jnp
from jax import lax
from jax.experimental import pallas as pl
from jax.experimental.pallas import tpu as pltpu
from jax.sharding import PartitionSpec as P


AXES = ("lat", "lon")
F32 = jnp.float32
BF16 = jnp.bfloat16
LANES = 128
OFF = 8
VMEM = pl.BlockSpec(memory_space=pltpu.VMEM)
SMEM = pl.BlockSpec(memory_space=pltpu.SMEM)
HBM = pl.BlockSpec(memory_space=pl.ANY)


def iota(shape, dim):
    return lax.broadcasted_iota(jnp.int32, shape, dim)


BIG = 4 << 20


def nbytes(shape, dtype):
    return math.prod(shape) * jnp.dtype(dtype).itemsize


def call(body, outs, in_specs, scratch=(), aliases=None, keep=True):
    def placed(s, d):
        return pltpu.VMEM(s, d) if keep and nbytes(s, d) <= BIG else jax.ShapeDtypeStruct(s, d)

    def apply(*args):
        own = sum(nbytes(x.shape, x.dtype) for x in scratch if getattr(x, "memory_space", None) == pltpu.VMEM)
        own += sum(nbytes(x.shape, x.dtype) for x in args if nbytes(x.shape, x.dtype) > BIG)
        own += sum(nbytes(s, d) for s, d in outs if not keep or nbytes(s, d) > BIG)
        run = pl.pallas_call(
            body,
            out_shape=[placed(s, d) for s, d in outs],
            in_specs=in_specs,
            out_specs=[VMEM] * len(outs),
            scratch_shapes=list(scratch),
            input_output_aliases=aliases or {},
            compiler_params=pltpu.CompilerParams(vmem_limit_bytes=own + (6 << 20)),
        )

        def place(x, spec):
            if spec is HBM:
                return pltpu.with_memory_space_constraint(x, pltpu.HBM)
            if spec is VMEM and nbytes(x.shape, x.dtype) <= BIG:
                return pltpu.with_memory_space_constraint(x, pltpu.VMEM)
            return x

        return run(*(place(x, spec) for x, spec in zip(args, in_specs)))

    return apply


def split3(x):
    hi = x.astype(BF16).astype(F32)
    rest = x - hi
    mid = rest.astype(BF16).astype(F32)
    return hi, mid, rest - mid


def border_rows(field, rates):
    trc, lev, rows, _ = field.shape
    tiles = trc * lev

    def body(f, t, up, down, f_last, f_first, t_last, t_first, sem):
        moves = [
            pltpu.make_async_copy(src.at[:, pl.ds(at, 2), :], dst.at[:, pl.ds(0, 2), :], sem.at[i])
            for i, (src, at, dst) in enumerate(
                ((f, rows - 2, f_last), (f, 0, f_first), (t, rows - 2, t_last), (t, 0, t_first)))
        ]
        for move in moves:
            move.start()

        def row(ref, group, at):
            return ref.reshape(ref.shape[0] * 8, LANES)[pl.ds(group * lev * 8 + at, lev, stride=8), :]

        moves[0].wait()
        for k in range(trc):
            up[k] = row(f_last, k, 0)
            up[trc + k] = row(f_last, k, 1)
        moves[1].wait()
        for k in range(trc):
            down[k] = row(f_first, k, 1)
            down[trc + k] = row(f_first, k, 0)
        moves[2].wait()
        for d in range(6):
            up[2 * trc + d] = row(t_last, d, 1)
        moves[3].wait()
        for d in range(6):
            down[2 * trc + d] = row(t_first, d, 0)

    out = ((2 * trc + 6, lev, LANES), F32)
    return call(
        body,
        [out, out],
        [HBM, HBM],
        [pltpu.VMEM((n, 8, LANES), F32) for n in (tiles, tiles, 6 * lev, 6 * lev)] + [pltpu.SemaphoreType.DMA((4,))],
    )(field.reshape(tiles, rows, LANES), rates.reshape(6 * lev, rows, LANES))


def border_cols(field, rates):
    trc, lev, rows, _ = field.shape
    tiles = trc * lev

    def body(f, t, east, west):
        lane = iota((8, LANES), 1)
        east[pl.ds(2 * rows, 8), :] = jnp.zeros((8, LANES), F32)
        west[pl.ds(2 * rows, 8), :] = jnp.zeros((8, LANES), F32)
        for c in range(0, rows, 8):
            e = jnp.zeros((8, LANES), F32)
            w = jnp.zeros((8, LANES), F32)
            for m in range(tiles):
                v = f[m, pl.ds(c, 8), :]
                e = jnp.where(lane == m, pltpu.roll(v, (m - 127) % LANES, 1), e)
                e = jnp.where(lane == 64 + m, pltpu.roll(v, (64 + m - 126) % LANES, 1), e)
                w = jnp.where(lane == m, pltpu.roll(v, m % LANES, 1), w)
                w = jnp.where(lane == 64 + m, pltpu.roll(v, (64 + m - 1) % LANES, 1), w)
            east[pl.ds(c, 8), :] = e
            west[pl.ds(c, 8), :] = w
            e = jnp.zeros((8, LANES), F32)
            w = jnp.zeros((8, LANES), F32)
            for j in range(6 * lev):
                v = t[j, pl.ds(c, 8), :]
                e = jnp.where(lane == j, pltpu.roll(v, (j - 127) % LANES, 1), e)
                w = jnp.where(lane == j, pltpu.roll(v, j % LANES, 1), w)
            east[pl.ds(rows + c, 8), :] = e
            west[pl.ds(rows + c, 8), :] = w

    return call(body, [((2 * rows + 8, LANES), F32)] * 2, [VMEM, VMEM])(
        field.reshape(tiles, rows, LANES), rates.reshape(6 * lev, rows, LANES))


def masks(band, bands):
    south = jnp.where(band > 0, 1.0, 0.0).astype(F32)
    north = jnp.where(band < bands - 1, 1.0, 0.0).astype(F32)
    return south, north


def corners(east, west, before, after, bands):
    rows = (east.shape[0] - 8) // 2
    lev = before.shape[1]
    trc = (before.shape[0] - 6) // 2

    def body(east_in, west_in, b, a, e_ref, w_ref):
        lane, sub = iota((lev, LANES), 1), iota((lev, LANES), 0)
        e_ref[...] = east_in[...]
        w_ref[...] = west_in[...]
        for which, (ref, mask) in enumerate(zip((b, a), masks(lax.axis_index("lat"), bands))):
            to_e = jnp.zeros((lev, LANES), F32)
            to_w = jnp.zeros((lev, LANES), F32)
            for k in range(trc):
                v = ref[trc + k] * mask
                here = lane == k * lev + sub
                to_e = jnp.where(here, jnp.broadcast_to(v[:, LANES - 1 :], v.shape), to_e)
                to_w = jnp.where(here, jnp.broadcast_to(v[:, :1], v.shape), to_w)
            e_ref[pl.ds(2 * rows + which, 1), :] = jnp.sum(to_e, axis=0, keepdims=True)
            w_ref[pl.ds(2 * rows + which, 1), :] = jnp.sum(to_w, axis=0, keepdims=True)

    return call(body, [(x.shape, F32) for x in (east, west)], [VMEM] * 4)(
        east, west, before, after)


def centre(rate):
    return 1.0 - rate[0] - rate[1] - rate[2] - rate[3] - rate[4] - rate[5]


def edge_rates(ref, trc, lev):
    sub = iota((lev, LANES), 0)
    rate = [ref[2 * trc + d] for d in range(6)]
    rate[4] = jnp.where(sub < lev - 1, rate[4], 0.0)
    rate[5] = jnp.where(sub > 0, rate[5], 0.0)
    return rate, centre(rate)


def stencil(load, mids, tv, lev, rows, emit):
    for l in range(lev):
        for r in range(0, rows, 8):
            rate = [tv[d * lev + l, pl.ds(r, 8), :] for d in range(6)]
            c = load(l, r, 0)
            west, east = pltpu.roll(c, 1, 1), pltpu.roll(c, LANES - 1, 1)
            v = mids[l, pl.ds(r, 8), :] * c + rate[2] * load(l, r, 1) + rate[3] * load(l, r, -1)
            if l < lev - 1:
                v = v + rate[4] * load(l + 1, r, 0)
            if l > 0:
                v = v + rate[5] * load(l - 1, r, 0)
            emit(l, r, v, rate, west, east)


def first_step(bands, field, rates, before, after, up, down, trc, lev, rows):
    high = rows + 2 * OFF
    tiles = trc * lev

    def body(f, tv, b, a, my_up, my_down, f1, mids):
        lane, edge = iota((8, LANES), 1), iota((8, LANES), 0)
        lane_l = iota((lev, LANES), 1)
        flat = f1.reshape(tiles * high, LANES)
        bf, af = (x.reshape((2 * trc + 6) * lev, LANES) for x in (b, a))
        south_mask, north_mask = masks(lax.axis_index("lat"), bands)
        for which, (ref, mine, mask) in enumerate(zip((b, a), (my_down, my_up), (south_mask, north_mask))):
            rate, mid = edge_rates(ref, trc, lev)
            for k in range(trc):
                c = ref[trc + k]
                far, own = ref[k], mine[trc + k]
                north, south = (own, far) if which == 0 else (far, own)
                east = jnp.where(lane_l == LANES - 1, 0.0, pltpu.roll(c, LANES - 1, 1))
                west = jnp.where(lane_l == 0, 0.0, pltpu.roll(c, 1, 1))
                g = (mid * c + rate[0] * east + rate[1] * west + rate[2] * north + rate[3] * south
                     + rate[4] * pltpu.roll(c, lev - 1, 0) + rate[5] * pltpu.roll(c, 1, 0))
                at = OFF - 1 if which == 0 else OFF + rows
                flat[pl.ds(k * lev * high + at, lev, stride=high), :] = g * mask
        for l in range(lev):
            for r in range(0, rows, 8):
                rate = [tv[d * lev + l, pl.ds(r, 8), :] for d in range(6)]
                if l == lev - 1:
                    rate[4] = jnp.zeros_like(rate[4])
                if l == 0:
                    rate[5] = jnp.zeros_like(rate[5])
                mids[l, pl.ds(r, 8), :] = centre(rate)

        def tracer(k, carry):
            def load(l, r, by):
                m = k * lev + l
                if r + by < 0:
                    ghost = bf[pl.ds((trc + k) * lev + l, 8, stride=0), :] * south_mask
                    return jnp.where(edge == 0, ghost, pltpu.roll(f[m, pl.ds(0, 8), :], 1, 0))
                if r + by + 8 > rows:
                    ghost = af[pl.ds((trc + k) * lev + l, 8, stride=0), :] * north_mask
                    return jnp.where(edge == 7, ghost, pltpu.roll(f[m, pl.ds(rows - 8, 8), :], 7, 0))
                return f[m, pl.ds(r + by, 8), :]

            def emit(l, r, v, rate, west, east):
                f1[k * lev + l, pl.ds(OFF + r, 8), :] = v + (
                    rate[0] * jnp.where(lane == LANES - 1, 0.0, east) + rate[1] * jnp.where(lane == 0, 0.0, west))

            stencil(load, mids, tv, lev, rows, emit)
            return carry

        lax.fori_loop(0, trc, tracer, 0)

    return call(body, [((tiles, high, LANES), F32), ((lev, rows, LANES), F32)], [VMEM] * 6)(
        field.reshape(tiles, rows, LANES), rates.reshape(6 * lev, rows, LANES), before, after, up, down)


def transport_kernel(trc, lev, rows, bands, f1, mids, tv, w_in, e_in, my_east, my_west, b, a,
                     lam, level0, row_sums, whole, cols, ghost0, ghost1, halves):
    high = rows + 2 * OFF
    lane = iota((8, LANES), 1)
    sub = iota((lev, LANES), 0)
    lane_l = iota((lev, LANES), 1)
    f1_flat = f1.reshape(trc * lev * high, LANES)
    whole_flat = whole.reshape(lev * high, LANES)
    level_of = lane % lev
    from_west, from_east = lane // 2, (lane + 1) // 2 % 64

    def ghosts(west, east):
        return jnp.where(lane % 2 == 0, jnp.take_along_axis(west, from_west, axis=1),
                         jnp.take_along_axis(east, from_east, axis=1))

    for side, ref in enumerate((w_in, e_in)):
        cols[side, pl.ds(OFF, rows), :] = ref[pl.ds(0, rows), :]
        cols[side, pl.ds(OFF - 1, 1), :] = ref[pl.ds(2 * rows, 1), :]
        cols[side, pl.ds(OFF + rows, 1), :] = ref[pl.ds(2 * rows + 1, 1), :]
    for r in range(0, rows, 8):
        stepped = []
        for side, (ref, mine) in enumerate(((w_in, my_west), (e_in, my_east))):
            c = cols[side, pl.ds(OFF + r, 8), :]
            north, south = cols[side, pl.ds(OFF + r + 1, 8), :], cols[side, pl.ds(OFF + r - 1, 8), :]
            far, own = pltpu.roll(c, 64, 1), mine[pl.ds(r, 8), :]
            east, west = (own, far) if side == 0 else (far, own)
            packed = ref[pl.ds(rows + r, 8), :]
            rate = [jnp.take_along_axis(packed, d * lev + level_of, axis=1) for d in range(6)]
            rate[4] = jnp.where(level_of < lev - 1, rate[4], 0.0)
            rate[5] = jnp.where(level_of > 0, rate[5], 0.0)
            upper, lower = pltpu.roll(c, LANES - 1, 1), pltpu.roll(c, 1, 1)
            stepped.append(centre(rate) * c + rate[0] * east + rate[1] * west + rate[2] * north + rate[3] * south
                           + rate[4] * upper + rate[5] * lower)
        ghost0[pl.ds(r, 8), :] = ghosts(w_in[pl.ds(r, 8), :], e_in[pl.ds(r, 8), :])
        ghost1[pl.ds(r, 8), :] = ghosts(*stepped)
    side_masks = masks(lax.axis_index("lat"), bands)

    def tracer(k, carry):
        def beside(ghost, l, r):
            return pltpu.roll(ghost[pl.ds(r, 8), :], (LANES - 2 * (k * lev + l)) % LANES, 1)

        def ends(at, west, east):
            return jnp.where(at == 0, west, jnp.where(at == LANES - 1, east, 0.0))

        for which, (ref, mask) in enumerate(zip((b, a), side_masks)):
            at = OFF - 1 if which == 0 else OFF + rows
            corner = [jnp.take_along_axis(
                jnp.broadcast_to(x[pl.ds(2 * rows + which, 1), :], (lev, LANES)), k * lev + sub, axis=1)
                for x in (w_in, e_in)]
            more = ends(lane_l, ref[2 * trc + 1] * corner[0], ref[2 * trc] * corner[1])
            whole_flat[pl.ds(at, lev, stride=high), :] = (
                f1_flat[pl.ds(k * lev * high + at, lev, stride=high), :] + more * mask)
        for l in range(lev):
            for r in range(0, rows, 8):
                g = beside(ghost0, l, r)
                whole[l, pl.ds(OFF + r, 8), :] = f1[k * lev + l, pl.ds(OFF + r, 8), :] + ends(
                    lane, tv[lev + l, pl.ds(r, 8), :] * g, tv[l, pl.ds(r, 8), :] * g)

        def emit(l, r, v, rate, west, east):
            g = beside(ghost1, l, r)
            v = v + (rate[0] * jnp.where(lane == LANES - 1, g, east) + rate[1] * jnp.where(lane == 0, g, west))
            lam[k * lev + l, pl.ds(r, 8), :] = v
            if l == 0:
                level0[pl.ds(r * trc + k, 8, stride=trc), :] = v

        stencil(lambda l, r, by: whole[l, pl.ds(OFF + r + by, 8), :], mids, tv, lev, rows, emit)
        for l in range(lev):
            for r in range(0, rows, 16):
                v = lam[k * lev + l, pl.ds(r, 16), :]
                hi = v.astype(BF16)
                halves[k, pl.ds(l * rows + r, 16), pl.ds(0, LANES)] = hi
                halves[k, pl.ds(l * rows + r, 16), pl.ds(LANES, LANES)] = (v - hi.astype(F32)).astype(BF16)
        return carry

    lax.fori_loop(0, trc, tracer, 0)
    total = [jnp.zeros((8, LANES), F32) for _ in range(0, rows, 8)]
    ones = jnp.ones((2 * LANES, LANES), BF16)
    for k in range(trc):
        sums = jnp.dot(halves[k], ones, preferred_element_type=F32)
        for l in range(lev):
            for i in range(rows // 8):
                at = l * rows + 8 * i
                total[i] = jnp.where(lane == l * trc + k, sums[at : at + 8], total[i])
    for i in range(rows // 8):
        row_sums[pl.ds(8 * i, 8), :] = total[i]


def transport(bands, f1, mids, rates, w_in, e_in, east, west, before, after, trc, lev, rows):
    high = rows + 2 * OFF
    return call(
        functools.partial(transport_kernel, trc, lev, rows, bands),
        [((trc * lev, rows, LANES), F32), ((rows * trc, LANES), F32), ((rows, LANES), F32)],
        [VMEM] * 9,
        [
            pltpu.VMEM((lev, high, LANES), F32),
            pltpu.VMEM((2, high, LANES), F32),
            pltpu.VMEM((rows, LANES), F32),
            pltpu.VMEM((rows, LANES), F32),
            pltpu.VMEM((trc, lev * rows, 2 * LANES), BF16),
        ],
    )(f1, mids, rates.reshape(6 * lev, rows, LANES), w_in, e_in, east, west, before, after)


def numbered(row, each, blocks):
    return (row & (blocks - 1)) * each + (row >> (blocks.bit_length() - 1))


def tables(region_local, cell_weight, polar_rows, local, blocks):
    rows, cols = region_local.shape

    def body(rl, w_ref, p_ref, hot, zc, half, w1, wz):
        eye = iota((rows, rows), 0) == iota((rows, rows), 1)
        flags = jnp.broadcast_to(p_ref[...].astype(F32), (rows, rows))
        hp = 0.5 * jnp.sum(jnp.where(eye, flags, 0.0), axis=1, keepdims=True)
        hp = jnp.broadcast_to(hp, (rows, cols))
        half[...] = hp
        w = w_ref[...]
        w1[...] = w * (1.0 - hp)
        w1z = split3(w * hp)
        row_id = iota((rows, cols), 0)
        entry = numbered(iota((local, cols), 0), local // blocks, blocks)
        for r in range(rows):
            hot[:, pl.ds(r * cols, cols)] = (rl[pl.ds(r, 1), :] == entry).astype(F32).astype(BF16)
            for i in range(3):
                wz[pl.ds(i * rows, rows), pl.ds(r * cols, cols)] = jnp.where(row_id == r, w1z[i], 0.0).astype(BF16)
        z = lax.dot_general(wz[...], hot[...], (((1,), (1,)), ((), ())), preferred_element_type=F32)
        z = z[:rows] + z[rows : 2 * rows] + z[2 * rows :]
        hi, mid, lo = split3(jnp.concatenate([z, jnp.zeros((LANES - rows, local), F32)], axis=0))
        for i, piece in enumerate((hi, mid, lo)):
            turned = jnp.transpose(piece)[:, :rows].astype(BF16)
            for at in ((0, 3, 5), (1, 4), (2,))[i]:
                zc[:, pl.ds(at * rows, rows)] = turned

    return call(
        body,
        [((local, rows * cols), BF16), ((local, 6 * rows), BF16), ((rows, cols), F32), ((rows, cols), F32)],
        [VMEM] * 3,
        [pltpu.VMEM((3 * rows, rows * cols), BF16)],
    )(region_local, cell_weight, polar_rows.reshape(1, rows))


def places(tile_regions, own_rows):
    count, local = tile_regions.shape
    regions = own_rows * count
    blocks = regions // LANES
    each = local // blocks
    width = count * each
    group = LANES // each

    def body(tr, out):
        lane, sub = iota((group, LANES), 1), iota((group, LANES), 0)
        region = iota((LANES, LANES), 0)

        def block(q, carry):
            first = q * each
            src_at = pl.multiple_of(first // LANES * LANES, LANES)
            from_lane = first % LANES + lane % each
            for g in range(width // LANES):
                src = tr[pl.ds(g * group, group), pl.ds(src_at, LANES)]
                got = jnp.take_along_axis(src, from_lane, axis=1)
                row = jnp.sum(jnp.where(lane // each == sub, got, 0), axis=0, keepdims=True)
                out[pl.ds(pl.multiple_of(q * LANES, LANES), LANES), pl.ds(g * LANES, LANES)] = (
                    (row == q * LANES + region).astype(F32).astype(BF16))
            return carry

        lax.fori_loop(0, blocks, block, 0)

    return call(body, [((regions, width), BF16)], [VMEM])(tile_regions)[0]


def local_sums(level0, w1, hot):
    rows, cols = w1.shape
    trc = level0.shape[0] // rows
    local = hot.shape[0]

    def body(l0, w, hot_ref, out, lhs):
        for r in range(rows):
            s = l0[pl.ds(r * trc, trc), :] * w[pl.ds(r, 1), :]
            hi, mid, lo = split3(s)
            at = pl.ds(r * cols, cols)
            lhs[pl.ds(0, 2 * trc), at] = jnp.concatenate([hi, mid], axis=0).astype(BF16)
            lhs[pl.ds(2 * trc, 2 * trc), at] = jnp.concatenate([lo, jnp.zeros_like(lo)], axis=0).astype(BF16)
        s = lax.dot_general(lhs[...], hot_ref[...], (((1,), (1,)), ((), ())), preferred_element_type=F32)
        s = s[:trc] + s[trc : 2 * trc] + s[2 * trc : 3 * trc]
        out[...] = jnp.transpose(jnp.concatenate([s, jnp.zeros((LANES - trc, local), F32)], axis=0))

    return call(
        body, [((local, LANES), F32)], [VMEM] * 3, [pltpu.VMEM((4 * trc, rows * cols), BF16)]
    )(level0, w1, hot)[0]


def regional(parts, s1, zc, trc, devices, columns, blocks):
    rows, _ = parts[0].shape
    local = s1.shape[0]
    each, width = local // blocks, blocks * trc

    def body(*refs):
        ins, (s_ref, zc_ref, zonal, out, mixed) = refs[: len(parts)], refs[len(parts) :]
        z = ins[0][...]
        for ref in ins[1:]:
            z = z + ref[...]
        z = z / columns
        zonal[...] = z
        hi, mid, lo = split3(z)
        pieces = jnp.concatenate([x.astype(BF16) for x in (hi, hi, hi, mid, mid, lo)], axis=0)
        more = jnp.dot(zc_ref[...], pieces, preferred_element_type=F32)
        mixed[...] = s_ref[...] + jnp.where(iota((local, LANES), 1) < trc, more, 0.0)
        for c in range(0, width, LANES):
            total = jnp.zeros((each, LANES), F32)
            for q in range(c // trc, (c + LANES) // trc):
                total = total + pltpu.roll(mixed[pl.ds(q, each, stride=blocks), :], q * trc % LANES, 1)
            for d in range(devices):
                out[d, :, pl.ds(c, LANES)] = total

    return call(
        body, [((rows, LANES), F32), ((devices, each, width), F32)], [VMEM] * (len(parts) + 2),
        [pltpu.VMEM((local, LANES), F32)]
    )(*parts, s1, zc)


def filtered(lam, zonal, half, trc, lev):
    tiles, rows, _ = lam.shape

    def body(l_ref, z_ref, h_ref, out):
        for r in range(0, rows, 8):
            z, h = z_ref[pl.ds(r, 8), :], h_ref[pl.ds(r, 8), :]
            for m in range(tiles):
                i = m % lev * trc + m // lev
                v = l_ref[m, pl.ds(r, 8), :]
                out[m, pl.ds(r, 8), :] = v + h * (jnp.broadcast_to(z[:, i : i + 1], v.shape) - v)

    return call(body, [(lam.shape, F32)], [VMEM] * 3, keep=False)(lam, zonal, half)[0]


def finish(week, sums, hot, cov, base, trc):
    own_rows, _ = cov.shape
    cols = base.shape[1]
    width = sums.shape[1]
    span = LANES // trc * LANES

    def body(week_ref, s_ref, hot_ref, cov_ref, base_ref, out):
        added = jnp.zeros((own_rows, LANES), F32)
        for c in range(0, width, LANES):
            parts = [x.astype(BF16) for x in split3(jnp.transpose(s_ref[:, pl.ds(c, LANES)]))]
            fresh = []
            for q in range(0, LANES // trc, 2):
                rows = slice(q * trc, (q + 2) * trc)
                both = lax.dot_general(
                    jnp.concatenate([x[rows] for x in parts], axis=0),
                    hot_ref[pl.ds((c // trc + q) * LANES, 2 * LANES), :],
                    (((1,), (1,)), ((), ())), preferred_element_type=F32)
                both = both[: 2 * trc] + both[2 * trc : 4 * trc] + both[4 * trc :]
                fresh += [both[:trc, :LANES], both[trc:, LANES:]]
            fresh = jnp.concatenate(fresh, axis=1)
            fresh = jnp.concatenate([fresh] * (LANES // trc), axis=0).astype(BF16)
            added = added + lax.dot_general(
                cov_ref[:, pl.ds(c // trc * LANES, span)], fresh, (((1,), (1,)), ((), ())),
                preferred_element_type=F32)
        for c in range(0, cols, LANES):
            w = min(LANES, cols - c)
            here = (c + iota((own_rows, LANES), 1)) // trc == week_ref[0]
            out[:, pl.ds(c, w)] = base_ref[:, pl.ds(c, w)] + jnp.where(here, added, 0.0)[:, :w]

    return call(body, [((own_rows, cols), F32)], [SMEM] + [VMEM] * 4, keep=False)(
        week, sums, hot, cov, base)[0]


def ring(size):
    up = [(i, (i + 1) % size) for i in range(size)]
    return up, [(j, i) for i, j in up]


def partners(devices, bit):
    return [(i, i ^ bit) for i in range(devices)]


def append(parts, cols):
    rows = sum(x.shape[0] for x in parts)

    def body(*refs):
        at = 0
        for ref in refs[:-1]:
            here = pl.ds(at, ref.shape[0])
            refs[-1][here, pl.ds(0, ref.shape[1])] = ref[...]
            if cols > ref.shape[1]:
                refs[-1][here, pl.ds(ref.shape[1], cols - ref.shape[1])] = jnp.zeros(
                    (ref.shape[0], cols - ref.shape[1]), ref.dtype)
            at += ref.shape[0]

    return call(body, [((rows, cols), parts[0].dtype)], [VMEM] * len(parts))(*parts)[0]


def base_product(mine, theirs, cov, turn, cols):
    own_rows, regions = cov.shape
    wide = mine.shape[1]
    half = len(turn) // 2

    def body(a, b, cov_ref, out, grad):
        tile = lax.axis_index("lat") * lax.axis_size("lon") + lax.axis_index("lon")
        for j, flip in enumerate(turn):
            src = a if j < half else b
            at = pl.multiple_of((tile ^ flip) * own_rows, own_rows)
            grad[pl.ds(at, own_rows), :] = src[pl.ds(j % half * own_rows, own_rows), :]
        out[...] = jnp.dot(cov_ref[...], grad[...], preferred_element_type=F32)[:, :cols]

    return call(
        body, [((own_rows, cols), F32)], [VMEM] * 3, [pltpu.VMEM((regions, wide), cov.dtype)]
    )(mine, theirs, cov)[0]


def shards(adjoint, transport_rates, cell_weight, region_local, tile_regions, polar_rows, week_index, grad_in, covariance):
    trc, lev, rows, cols = adjoint.shape
    own_rows, regions = covariance.shape
    lats, lons = lax.axis_size("lat"), lax.axis_size("lon")
    devices = lats * lons
    north_to, south_to = ring(lats)
    east_to, west_to = ring(lons)

    lon_bits, bits = lons.bit_length() - 1, devices.bit_length() - 1
    far = list(range(lon_bits + 1, bits))
    order = list(range(lon_bits - 1, 0, -1)) + far[:1] + [0] + far[1:] + [lon_bits]
    turn = [0]
    for bit in order:
        turn = turn + [j ^ (1 << bit) for j in turn]

    def exchange(i, x):
        return lax.ppermute(x, AXES, partners(devices, 1 << order[i]))

    have = grad_in
    for i in range(len(order) - 1):
        wide = pl.cdiv(have.shape[1], LANES) * LANES if i == len(order) - 2 else have.shape[1]
        have = append([have, exchange(i, have)], wide)
    theirs = exchange(len(order) - 1, have)

    up, down = border_rows(adjoint, transport_rates)
    before = lax.ppermute(up, "lat", north_to)
    after = lax.ppermute(down, "lat", south_to)
    east, west = border_cols(adjoint, transport_rates)
    east, west = corners(east, west, before, after, lats)
    w_in = lax.ppermute(east, "lon", east_to)
    e_in = lax.ppermute(west, "lon", west_to)
    blocks = regions // LANES
    hot, zc, half, w1 = tables(region_local, cell_weight, polar_rows, tile_regions.shape[1], blocks)
    where = places(tile_regions, own_rows)
    f1, mids = first_step(lats, adjoint, transport_rates, before, after, up, down, trc, lev, rows)
    lam, level0, row_sums = transport(
        lats, f1, mids, transport_rates, w_in, e_in, east, west, before, after, trc, lev, rows)

    if lons <= 4:
        parts = [row_sums] + [lax.ppermute(row_sums, "lon", partners(lons, k)) for k in range(1, lons)]
    else:
        got = lax.all_to_all(
            jnp.broadcast_to(row_sums[None], (lons,) + row_sums.shape), "lon", 0, 0, tiled=True)
        parts = [jnp.sum(got, axis=0)]
    s1 = local_sums(level0, w1, hot)
    zonal, copies = regional(parts, s1, zc, trc, devices, cols * lons, blocks)
    sums = lax.all_to_all(copies, AXES, 0, 0, tiled=True)
    sums = sums.reshape(-1, sums.shape[2])
    adjoint_out = filtered(lam, zonal, half, trc, lev).reshape(adjoint.shape)
    base = base_product(have, theirs, covariance, turn, grad_in.shape[1])
    precond = finish(week_index, sums, where, covariance, base, trc)
    return adjoint_out, precond


def solution(mesh):
    in_specs = (
        P(None, None, "lat", "lon"),
        P(None, None, "lat", "lon"),
        P("lat", "lon"),
        P("lat", "lon"),
        P(),
        P("lat"),
        P(),
        P(("lat", "lon"), None),
        P(("lat", "lon"), None),
    )
    out_specs = (P(None, None, "lat", "lon"), P(("lat", "lon"), None))
    return jax.shard_map(shards, mesh=mesh, in_specs=in_specs, out_specs=out_specs, check_vma=False)
```

```python
import functools
import math

import jax
import jax.numpy as jnp
from jax import lax
from jax.experimental import pallas as pl
from jax.experimental.pallas import tpu as pltpu
from jax.sharding import PartitionSpec as P


AXES = ("lat", "lon")
F32 = jnp.float32
BF16 = jnp.bfloat16
LANES = 128
OFF = 8
VMEM = pl.BlockSpec(memory_space=pltpu.VMEM)
SMEM = pl.BlockSpec(memory_space=pltpu.SMEM)
HBM = pl.BlockSpec(memory_space=pl.ANY)


def iota(shape, dim):
    return lax.broadcasted_iota(jnp.int32, shape, dim)


BIG = 4 << 20


def nbytes(shape, dtype):
    return math.prod(shape) * jnp.dtype(dtype).itemsize


def call(body, outs, in_specs, scratch=(), aliases=None, keep=True):
    def placed(s, d):
        return pltpu.VMEM(s, d) if keep and nbytes(s, d) <= BIG else jax.ShapeDtypeStruct(s, d)

    def apply(*args):
        own = sum(nbytes(x.shape, x.dtype) for x in scratch if getattr(x, "memory_space", None) == pltpu.VMEM)
        own += sum(nbytes(x.shape, x.dtype) for x in args if nbytes(x.shape, x.dtype) > BIG)
        own += sum(nbytes(s, d) for s, d in outs if not keep or nbytes(s, d) > BIG)
        run = pl.pallas_call(
            body,
            out_shape=[placed(s, d) for s, d in outs],
            in_specs=in_specs,
            out_specs=[VMEM] * len(outs),
            scratch_shapes=list(scratch),
            input_output_aliases=aliases or {},
            compiler_params=pltpu.CompilerParams(vmem_limit_bytes=own + (own // 2 if own > BIG else 0) + (6 << 20)),
        )

        def place(x, spec):
            if spec is HBM:
                return pltpu.with_memory_space_constraint(x, pltpu.HBM)
            if spec is VMEM and nbytes(x.shape, x.dtype) <= BIG:
                return pltpu.with_memory_space_constraint(x, pltpu.VMEM)
            return x

        return run(*(place(x, spec) for x, spec in zip(args, in_specs)))

    return apply


def split3(x):
    hi = x.astype(BF16).astype(F32)
    rest = x - hi
    mid = rest.astype(BF16).astype(F32)
    return hi, mid, rest - mid


def border_rows(field, rates):
    trc, lev, rows, _ = field.shape
    tiles = trc * lev

    def body(f, t, up, down, f_last, f_first, t_last, t_first, sem):
        moves = [
            pltpu.make_async_copy(src.at[:, pl.ds(at, 2), :], dst.at[:, pl.ds(0, 2), :], sem.at[i])
            for i, (src, at, dst) in enumerate(
                ((f, rows - 2, f_last), (f, 0, f_first), (t, rows - 2, t_last), (t, 0, t_first)))
        ]
        for move in moves:
            move.start()

        def row(ref, group, at):
            return ref.reshape(ref.shape[0] * 8, LANES)[pl.ds(group * lev * 8 + at, lev, stride=8), :]

        moves[0].wait()
        for k in range(trc):
            up[k] = row(f_last, k, 0)
            up[trc + k] = row(f_last, k, 1)
        moves[1].wait()
        for k in range(trc):
            down[k] = row(f_first, k, 1)
            down[trc + k] = row(f_first, k, 0)
        moves[2].wait()
        for d in range(6):
            up[2 * trc + d] = row(t_last, d, 1)
        moves[3].wait()
        for d in range(6):
            down[2 * trc + d] = row(t_first, d, 0)

    out = ((2 * trc + 6, lev, LANES), F32)
    return call(
        body,
        [out, out],
        [HBM, HBM],
        [pltpu.VMEM((n, 8, LANES), F32) for n in (tiles, tiles, 6 * lev, 6 * lev)] + [pltpu.SemaphoreType.DMA((4,))],
    )(field.reshape(tiles, rows, LANES), rates.reshape(6 * lev, rows, LANES))


def border_cols(field, rates):
    trc, lev, rows, _ = field.shape
    tiles = trc * lev

    def body(f, t, east, west):
        lane = iota((8, LANES), 1)
        east[pl.ds(2 * rows, 8), :] = jnp.zeros((8, LANES), F32)
        west[pl.ds(2 * rows, 8), :] = jnp.zeros((8, LANES), F32)
        for c in range(0, rows, 8):
            e = jnp.zeros((8, LANES), F32)
            w = jnp.zeros((8, LANES), F32)
            for m in range(tiles):
                v = f[m, pl.ds(c, 8), :]
                e = jnp.where(lane == m, pltpu.roll(v, (m - 127) % LANES, 1), e)
                e = jnp.where(lane == 64 + m, pltpu.roll(v, (64 + m - 126) % LANES, 1), e)
                w = jnp.where(lane == m, pltpu.roll(v, m % LANES, 1), w)
                w = jnp.where(lane == 64 + m, pltpu.roll(v, (64 + m - 1) % LANES, 1), w)
            east[pl.ds(c, 8), :] = e
            west[pl.ds(c, 8), :] = w
            e = jnp.zeros((8, LANES), F32)
            w = jnp.zeros((8, LANES), F32)
            for j in range(6 * lev):
                v = t[j, pl.ds(c, 8), :]
                e = jnp.where(lane == j, pltpu.roll(v, (j - 127) % LANES, 1), e)
                w = jnp.where(lane == j, pltpu.roll(v, j % LANES, 1), w)
            east[pl.ds(rows + c, 8), :] = e
            west[pl.ds(rows + c, 8), :] = w

    return call(body, [((2 * rows + 8, LANES), F32)] * 2, [VMEM, VMEM])(
        field.reshape(tiles, rows, LANES), rates.reshape(6 * lev, rows, LANES))


def masks(band, bands):
    south = jnp.where(band > 0, 1.0, 0.0).astype(F32)
    north = jnp.where(band < bands - 1, 1.0, 0.0).astype(F32)
    return south, north


def corners(east, west, before, after, bands):
    rows = (east.shape[0] - 8) // 2
    lev = before.shape[1]
    trc = (before.shape[0] - 6) // 2

    def body(east_in, west_in, b, a, e_ref, w_ref):
        lane, sub = iota((lev, LANES), 1), iota((lev, LANES), 0)
        e_ref[...] = east_in[...]
        w_ref[...] = west_in[...]
        for which, (ref, mask) in enumerate(zip((b, a), masks(lax.axis_index("lat"), bands))):
            to_e = jnp.zeros((lev, LANES), F32)
            to_w = jnp.zeros((lev, LANES), F32)
            for k in range(trc):
                v = ref[trc + k] * mask
                here = lane == k * lev + sub
                to_e = jnp.where(here, jnp.broadcast_to(v[:, LANES - 1 :], v.shape), to_e)
                to_w = jnp.where(here, jnp.broadcast_to(v[:, :1], v.shape), to_w)
            e_ref[pl.ds(2 * rows + which, 1), :] = jnp.sum(to_e, axis=0, keepdims=True)
            w_ref[pl.ds(2 * rows + which, 1), :] = jnp.sum(to_w, axis=0, keepdims=True)

    return call(body, [(x.shape, F32) for x in (east, west)], [VMEM] * 4)(
        east, west, before, after)


def centre(rate):
    return 1.0 - rate[0] - rate[1] - rate[2] - rate[3] - rate[4] - rate[5]


def edge_rates(ref, trc, lev):
    sub = iota((lev, LANES), 0)
    rate = [ref[2 * trc + d] for d in range(6)]
    rate[4] = jnp.where(sub < lev - 1, rate[4], 0.0)
    rate[5] = jnp.where(sub > 0, rate[5], 0.0)
    return rate, centre(rate)


def stencil(load, mids, tv, lev, rows, emit):
    for l in range(lev):
        for r in range(0, rows, 8):
            rate = [tv[d * lev + l, pl.ds(r, 8), :] for d in range(6)]
            c = load(l, r, 0)
            west, east = pltpu.roll(c, 1, 1), pltpu.roll(c, LANES - 1, 1)
            v = mids[l, pl.ds(r, 8), :] * c + rate[2] * load(l, r, 1) + rate[3] * load(l, r, -1)
            if l < lev - 1:
                v = v + rate[4] * load(l + 1, r, 0)
            if l > 0:
                v = v + rate[5] * load(l - 1, r, 0)
            emit(l, r, v, rate, west, east)


def first_step(bands, field, rates, before, after, up, down, trc, lev, rows):
    high = rows + 2 * OFF
    tiles = trc * lev

    def body(f, tv, b, a, my_up, my_down, f1, mids):
        lane, edge = iota((8, LANES), 1), iota((8, LANES), 0)
        lane_l = iota((lev, LANES), 1)
        flat = f1.reshape(tiles * high, LANES)
        bf, af = (x.reshape((2 * trc + 6) * lev, LANES) for x in (b, a))
        south_mask, north_mask = masks(lax.axis_index("lat"), bands)
        for which, (ref, mine, mask) in enumerate(zip((b, a), (my_down, my_up), (south_mask, north_mask))):
            rate, mid = edge_rates(ref, trc, lev)
            for k in range(trc):
                c = ref[trc + k]
                far, own = ref[k], mine[trc + k]
                north, south = (own, far) if which == 0 else (far, own)
                east = jnp.where(lane_l == LANES - 1, 0.0, pltpu.roll(c, LANES - 1, 1))
                west = jnp.where(lane_l == 0, 0.0, pltpu.roll(c, 1, 1))
                g = (mid * c + rate[0] * east + rate[1] * west + rate[2] * north + rate[3] * south
                     + rate[4] * pltpu.roll(c, lev - 1, 0) + rate[5] * pltpu.roll(c, 1, 0))
                at = OFF - 1 if which == 0 else OFF + rows
                flat[pl.ds(k * lev * high + at, lev, stride=high), :] = g * mask
        for l in range(lev):
            for r in range(0, rows, 8):
                rate = [tv[d * lev + l, pl.ds(r, 8), :] for d in range(6)]
                if l == lev - 1:
                    rate[4] = jnp.zeros_like(rate[4])
                if l == 0:
                    rate[5] = jnp.zeros_like(rate[5])
                mids[l, pl.ds(r, 8), :] = centre(rate)

        def tracer(k, carry):
            def load(l, r, by):
                m = k * lev + l
                if r + by < 0:
                    ghost = bf[pl.ds((trc + k) * lev + l, 8, stride=0), :] * south_mask
                    return jnp.where(edge == 0, ghost, pltpu.roll(f[m, pl.ds(0, 8), :], 1, 0))
                if r + by + 8 > rows:
                    ghost = af[pl.ds((trc + k) * lev + l, 8, stride=0), :] * north_mask
                    return jnp.where(edge == 7, ghost, pltpu.roll(f[m, pl.ds(rows - 8, 8), :], 7, 0))
                return f[m, pl.ds(r + by, 8), :]

            def emit(l, r, v, rate, west, east):
                f1[k * lev + l, pl.ds(OFF + r, 8), :] = v + (
                    rate[0] * jnp.where(lane == LANES - 1, 0.0, east) + rate[1] * jnp.where(lane == 0, 0.0, west))

            stencil(load, mids, tv, lev, rows, emit)
            return carry

        lax.fori_loop(0, trc, tracer, 0)

    return call(body, [((tiles, high, LANES), F32), ((lev, rows, LANES), F32)], [VMEM] * 6)(
        field.reshape(tiles, rows, LANES), rates.reshape(6 * lev, rows, LANES), before, after, up, down)


def transport_kernel(trc, lev, rows, bands, f1, mids, tv, w_in, e_in, my_east, my_west, b, a,
                     lam, level0, row_sums, whole, cols, ghost0, ghost1, halves):
    high = rows + 2 * OFF
    lane = iota((8, LANES), 1)
    sub = iota((lev, LANES), 0)
    lane_l = iota((lev, LANES), 1)
    f1_flat = f1.reshape(trc * lev * high, LANES)
    whole_flat = whole.reshape(lev * high, LANES)
    level_of = lane % lev
    from_west, from_east = lane // 2, (lane + 1) // 2 % 64

    def ghosts(west, east):
        return jnp.where(lane % 2 == 0, jnp.take_along_axis(west, from_west, axis=1),
                         jnp.take_along_axis(east, from_east, axis=1))

    for side, ref in enumerate((w_in, e_in)):
        cols[side, pl.ds(OFF, rows), :] = ref[pl.ds(0, rows), :]
        cols[side, pl.ds(OFF - 1, 1), :] = ref[pl.ds(2 * rows, 1), :]
        cols[side, pl.ds(OFF + rows, 1), :] = ref[pl.ds(2 * rows + 1, 1), :]
    for r in range(0, rows, 8):
        stepped = []
        for side, (ref, mine) in enumerate(((w_in, my_west), (e_in, my_east))):
            c = cols[side, pl.ds(OFF + r, 8), :]
            north, south = cols[side, pl.ds(OFF + r + 1, 8), :], cols[side, pl.ds(OFF + r - 1, 8), :]
            far, own = pltpu.roll(c, 64, 1), mine[pl.ds(r, 8), :]
            east, west = (own, far) if side == 0 else (far, own)
            packed = ref[pl.ds(rows + r, 8), :]
            rate = [jnp.take_along_axis(packed, d * lev + level_of, axis=1) for d in range(6)]
            rate[4] = jnp.where(level_of < lev - 1, rate[4], 0.0)
            rate[5] = jnp.where(level_of > 0, rate[5], 0.0)
            upper, lower = pltpu.roll(c, LANES - 1, 1), pltpu.roll(c, 1, 1)
            stepped.append(centre(rate) * c + rate[0] * east + rate[1] * west + rate[2] * north + rate[3] * south
                           + rate[4] * upper + rate[5] * lower)
        ghost0[pl.ds(r, 8), :] = ghosts(w_in[pl.ds(r, 8), :], e_in[pl.ds(r, 8), :])
        ghost1[pl.ds(r, 8), :] = ghosts(*stepped)
    side_masks = masks(lax.axis_index("lat"), bands)

    def tracer(k, carry):
        def beside(ghost, l, r):
            return pltpu.roll(ghost[pl.ds(r, 8), :], (LANES - 2 * (k * lev + l)) % LANES, 1)

        def ends(at, west, east):
            return jnp.where(at == 0, west, jnp.where(at == LANES - 1, east, 0.0))

        for which, (ref, mask) in enumerate(zip((b, a), side_masks)):
            at = OFF - 1 if which == 0 else OFF + rows
            corner = [jnp.take_along_axis(
                jnp.broadcast_to(x[pl.ds(2 * rows + which, 1), :], (lev, LANES)), k * lev + sub, axis=1)
                for x in (w_in, e_in)]
            more = ends(lane_l, ref[2 * trc + 1] * corner[0], ref[2 * trc] * corner[1])
            whole_flat[pl.ds(at, lev, stride=high), :] = (
                f1_flat[pl.ds(k * lev * high + at, lev, stride=high), :] + more * mask)
        for l in range(lev):
            for r in range(0, rows, 8):
                g = beside(ghost0, l, r)
                whole[l, pl.ds(OFF + r, 8), :] = f1[k * lev + l, pl.ds(OFF + r, 8), :] + ends(
                    lane, tv[lev + l, pl.ds(r, 8), :] * g, tv[l, pl.ds(r, 8), :] * g)

        def emit(l, r, v, rate, west, east):
            g = beside(ghost1, l, r)
            v = v + (rate[0] * jnp.where(lane == LANES - 1, g, east) + rate[1] * jnp.where(lane == 0, g, west))
            lam[k * lev + l, pl.ds(r, 8), :] = v
            if l == 0:
                level0[pl.ds(r * trc + k, 8, stride=trc), :] = v

        stencil(lambda l, r, by: whole[l, pl.ds(OFF + r + by, 8), :], mids, tv, lev, rows, emit)
        for l in range(lev):
            for r in range(0, rows, 16):
                v = lam[k * lev + l, pl.ds(r, 16), :]
                hi = v.astype(BF16)
                halves[k, pl.ds(l * rows + r, 16), pl.ds(0, LANES)] = hi
                halves[k, pl.ds(l * rows + r, 16), pl.ds(LANES, LANES)] = (v - hi.astype(F32)).astype(BF16)
        return carry

    lax.fori_loop(0, trc, tracer, 0)
    total = [jnp.zeros((8, LANES), F32) for _ in range(0, rows, 8)]
    ones = jnp.ones((2 * LANES, LANES), BF16)
    for k in range(trc):
        sums = jnp.dot(halves[k], ones, preferred_element_type=F32)
        for l in range(lev):
            for i in range(rows // 8):
                at = l * rows + 8 * i
                total[i] = jnp.where(lane == l * trc + k, sums[at : at + 8], total[i])
    for i in range(rows // 8):
        row_sums[pl.ds(8 * i, 8), :] = total[i]


def transport(bands, f1, mids, rates, w_in, e_in, east, west, before, after, trc, lev, rows):
    high = rows + 2 * OFF
    return call(
        functools.partial(transport_kernel, trc, lev, rows, bands),
        [((trc * lev, rows, LANES), F32), ((rows * trc, LANES), F32), ((rows, LANES), F32)],
        [VMEM] * 9,
        [
            pltpu.VMEM((lev, high, LANES), F32),
            pltpu.VMEM((2, high, LANES), F32),
            pltpu.VMEM((rows, LANES), F32),
            pltpu.VMEM((rows, LANES), F32),
            pltpu.VMEM((trc, lev * rows, 2 * LANES), BF16),
        ],
    )(f1, mids, rates.reshape(6 * lev, rows, LANES), w_in, e_in, east, west, before, after)


def numbered(row, each, blocks):
    return (row & (blocks - 1)) * each + (row >> (blocks.bit_length() - 1))


def tables(region_local, cell_weight, polar_rows, local, blocks):
    rows, cols = region_local.shape

    def body(rl, w_ref, p_ref, hot, zc, half, w1, wz):
        eye = iota((rows, rows), 0) == iota((rows, rows), 1)
        flags = jnp.broadcast_to(p_ref[...].astype(F32), (rows, rows))
        hp = 0.5 * jnp.sum(jnp.where(eye, flags, 0.0), axis=1, keepdims=True)
        hp = jnp.broadcast_to(hp, (rows, cols))
        half[...] = hp
        w = w_ref[...]
        w1[...] = w * (1.0 - hp)
        w1z = split3(w * hp)
        row_id = iota((rows, cols), 0)
        entry = numbered(iota((local, cols), 0), local // blocks, blocks)
        for r in range(rows):
            hot[:, pl.ds(r * cols, cols)] = (rl[pl.ds(r, 1), :] == entry).astype(F32).astype(BF16)
            for i in range(3):
                wz[pl.ds(i * rows, rows), pl.ds(r * cols, cols)] = jnp.where(row_id == r, w1z[i], 0.0).astype(BF16)
        z = lax.dot_general(wz[...], hot[...], (((1,), (1,)), ((), ())), preferred_element_type=F32)
        z = z[:rows] + z[rows : 2 * rows] + z[2 * rows :]
        hi, mid, lo = split3(jnp.concatenate([z, jnp.zeros((LANES - rows, local), F32)], axis=0))
        for i, piece in enumerate((hi, mid, lo)):
            turned = jnp.transpose(piece)[:, :rows].astype(BF16)
            for at in ((0, 3, 5), (1, 4), (2,))[i]:
                zc[:, pl.ds(at * rows, rows)] = turned

    return call(
        body,
        [((local, rows * cols), BF16), ((local, 6 * rows), BF16), ((rows, cols), F32), ((rows, cols), F32)],
        [VMEM] * 3,
        [pltpu.VMEM((3 * rows, rows * cols), BF16)],
    )(region_local, cell_weight, polar_rows.reshape(1, rows))


def places(tile_regions, own_rows):
    count, local = tile_regions.shape
    regions = own_rows * count
    blocks = regions // LANES
    each = local // blocks
    width = count * each
    group = LANES // each

    def body(tr, out):
        lane, sub = iota((group, LANES), 1), iota((group, LANES), 0)
        region = iota((LANES, LANES), 0)

        def block(q, carry):
            first = q * each
            src_at = pl.multiple_of(first // LANES * LANES, LANES)
            from_lane = first % LANES + lane % each
            for g in range(width // LANES):
                src = tr[pl.ds(g * group, group), pl.ds(src_at, LANES)]
                got = jnp.take_along_axis(src, from_lane, axis=1)
                row = jnp.sum(jnp.where(lane // each == sub, got, 0), axis=0, keepdims=True)
                out[pl.ds(pl.multiple_of(q * LANES, LANES), LANES), pl.ds(g * LANES, LANES)] = (
                    (row == q * LANES + region).astype(F32).astype(BF16))
            return carry

        lax.fori_loop(0, blocks, block, 0)

    return call(body, [((regions, width), BF16)], [VMEM])(tile_regions)[0]


def local_sums(level0, w1, hot):
    rows, cols = w1.shape
    trc = level0.shape[0] // rows
    local = hot.shape[0]

    def body(l0, w, hot_ref, out, lhs):
        for r in range(rows):
            s = l0[pl.ds(r * trc, trc), :] * w[pl.ds(r, 1), :]
            hi, mid, lo = split3(s)
            at = pl.ds(r * cols, cols)
            lhs[pl.ds(0, 2 * trc), at] = jnp.concatenate([hi, mid], axis=0).astype(BF16)
            lhs[pl.ds(2 * trc, 2 * trc), at] = jnp.concatenate([lo, jnp.zeros_like(lo)], axis=0).astype(BF16)
        s = lax.dot_general(lhs[...], hot_ref[...], (((1,), (1,)), ((), ())), preferred_element_type=F32)
        s = s[:trc] + s[trc : 2 * trc] + s[2 * trc : 3 * trc]
        out[...] = jnp.transpose(jnp.concatenate([s, jnp.zeros((LANES - trc, local), F32)], axis=0))

    return call(
        body, [((local, LANES), F32)], [VMEM] * 3, [pltpu.VMEM((4 * trc, rows * cols), BF16)]
    )(level0, w1, hot)[0]


def regional(parts, s1, zc, trc, devices, columns, blocks):
    rows, _ = parts[0].shape
    local = s1.shape[0]
    each, width = local // blocks, blocks * trc

    def body(*refs):
        ins, (s_ref, zc_ref, zonal, out, mixed) = refs[: len(parts)], refs[len(parts) :]
        z = ins[0][...]
        for ref in ins[1:]:
            z = z + ref[...]
        z = z / columns
        zonal[...] = z
        hi, mid, lo = split3(z)
        pieces = jnp.concatenate([x.astype(BF16) for x in (hi, hi, hi, mid, mid, lo)], axis=0)
        more = jnp.dot(zc_ref[...], pieces, preferred_element_type=F32)
        mixed[...] = s_ref[...] + jnp.where(iota((local, LANES), 1) < trc, more, 0.0)
        for c in range(0, width, LANES):
            total = jnp.zeros((each, LANES), F32)
            for q in range(c // trc, (c + LANES) // trc):
                total = total + pltpu.roll(mixed[pl.ds(q, each, stride=blocks), :], q * trc % LANES, 1)
            for d in range(devices):
                out[d, :, pl.ds(c, LANES)] = total

    return call(
        body, [((rows, LANES), F32), ((devices, each, width), F32)], [VMEM] * (len(parts) + 2),
        [pltpu.VMEM((local, LANES), F32)]
    )(*parts, s1, zc)


def filtered(lam, zonal, half, trc, lev):
    tiles, rows, _ = lam.shape

    def body(l_ref, z_ref, h_ref, out):
        for r in range(0, rows, 8):
            z, h = z_ref[pl.ds(r, 8), :], h_ref[pl.ds(r, 8), :]
            for m in range(tiles):
                i = m % lev * trc + m // lev
                v = l_ref[m, pl.ds(r, 8), :]
                out[m, pl.ds(r, 8), :] = v + h * (jnp.broadcast_to(z[:, i : i + 1], v.shape) - v)

    return call(body, [(lam.shape, F32)], [VMEM] * 3, keep=False)(lam, zonal, half)[0]


def finish(week, sums, hot, cov, base, more, trc):
    own_rows, _ = cov.shape
    cols = base.shape[1]
    width = sums.shape[1]
    span = LANES // trc * LANES

    def body(week_ref, s_ref, hot_ref, cov_ref, base_ref, more_ref, out):
        added = jnp.zeros((own_rows, LANES), F32)
        for c in range(0, width, LANES):
            parts = [x.astype(BF16) for x in split3(jnp.transpose(s_ref[:, pl.ds(c, LANES)]))]
            fresh = []
            for q in range(0, LANES // trc, 2):
                rows = slice(q * trc, (q + 2) * trc)
                both = lax.dot_general(
                    jnp.concatenate([x[rows] for x in parts], axis=0),
                    hot_ref[pl.ds((c // trc + q) * LANES, 2 * LANES), :],
                    (((1,), (1,)), ((), ())), preferred_element_type=F32)
                both = both[: 2 * trc] + both[2 * trc : 4 * trc] + both[4 * trc :]
                fresh += [both[:trc, :LANES], both[trc:, LANES:]]
            fresh = jnp.concatenate(fresh, axis=1)
            fresh = jnp.concatenate([fresh] * (LANES // trc), axis=0).astype(BF16)
            added = added + lax.dot_general(
                cov_ref[:, pl.ds(c // trc * LANES, span)], fresh, (((1,), (1,)), ((), ())),
                preferred_element_type=F32)
        for c in range(0, cols, LANES):
            w = min(LANES, cols - c)
            here = (c + iota((own_rows, LANES), 1)) // trc == week_ref[0]
            out[:, pl.ds(c, w)] = base_ref[:, pl.ds(c, w)] + more_ref[:, pl.ds(c, w)] + jnp.where(here, added, 0.0)[:, :w]

    return call(body, [((own_rows, cols), F32)], [SMEM] + [VMEM] * 5, keep=False)(
        week, sums, hot, cov, base, more)[0]


def ring(size):
    up = [(i, (i + 1) % size) for i in range(size)]
    return up, [(j, i) for i, j in up]


def partners(devices, bit):
    return [(i, i ^ bit) for i in range(devices)]


def append(parts, cols):
    rows = sum(x.shape[0] for x in parts)

    def body(*refs):
        at = 0
        for ref in refs[:-1]:
            here = pl.ds(at, ref.shape[0])
            refs[-1][here, pl.ds(0, ref.shape[1])] = ref[...]
            if cols > ref.shape[1]:
                refs[-1][here, pl.ds(ref.shape[1], cols - ref.shape[1])] = jnp.zeros(
                    (ref.shape[0], cols - ref.shape[1]), ref.dtype)
            at += ref.shape[0]

    return call(body, [((rows, cols), parts[0].dtype)], [VMEM] * len(parts))(*parts)[0]


def upper_half():
    tile = lax.axis_index("lat") * lax.axis_size("lon") + lax.axis_index("lon")
    return tile // (lax.axis_size("lat") * lax.axis_size("lon") // 2)


def far_columns(cov):
    own_rows, regions = cov.shape
    half = regions // 2

    def body(cov_ref, out):
        out[...] = cov_ref[:, pl.ds(pl.multiple_of((1 - upper_half()) * half, half), half)]

    return call(body, [((own_rows, half), cov.dtype)], [VMEM])(cov)[0]


def base_product(mine, theirs, cov, far, turn, cols):
    own_rows, regions = cov.shape
    wide = mine.shape[1]
    half = regions // 2
    count = len(turn)

    def body(a, b, cov_ref, far_ref, out, other, grad):
        tile = lax.axis_index("lat") * lax.axis_size("lon") + lax.axis_index("lon")
        for j, flip in enumerate(turn):
            src = a if j < count // 2 else b
            at = pl.multiple_of(((tile ^ flip) & (count - 1)) * own_rows, own_rows)
            grad[pl.ds(at, own_rows), :] = src[pl.ds(j % (count // 2) * own_rows, own_rows), :]
        near = cov_ref[:, pl.ds(pl.multiple_of(upper_half() * half, half), half)]
        both = jnp.dot(jnp.concatenate([near, far_ref[...]], axis=0), grad[...], preferred_element_type=F32)
        out[...] = both[:own_rows, :cols]
        other[...] = both[own_rows:, :cols]

    return call(
        body, [((own_rows, cols), F32)] * 2, [VMEM] * 4, [pltpu.VMEM((half, wide), cov.dtype)]
    )(mine, theirs, cov, far)


def shards(adjoint, transport_rates, cell_weight, region_local, tile_regions, polar_rows, week_index, grad_in, covariance):
    trc, lev, rows, cols = adjoint.shape
    own_rows, regions = covariance.shape
    lats, lons = lax.axis_size("lat"), lax.axis_size("lon")
    devices = lats * lons
    north_to, south_to = ring(lats)
    east_to, west_to = ring(lons)

    lon_bits, bits = lons.bit_length() - 1, devices.bit_length() - 1
    far = list(range(lon_bits + 1, bits))
    order = list(range(lon_bits - 1, 0, -1)) + far[:1] + [0] + far[1:-1] + [lon_bits]
    top = partners(devices, devices // 2)
    turn = [0]
    for bit in order:
        turn = turn + [j ^ (1 << bit) for j in turn]

    def exchange(i, x):
        return lax.ppermute(x, AXES, partners(devices, 1 << order[i]))

    have = grad_in
    for i in range(len(order) - 1):
        wide = pl.cdiv(have.shape[1], LANES) * LANES if i == len(order) - 2 else have.shape[1]
        have = append([have, exchange(i, have)], wide)
    theirs = exchange(len(order) - 1, have)

    up, down = border_rows(adjoint, transport_rates)
    before = lax.ppermute(up, "lat", north_to)
    after = lax.ppermute(down, "lat", south_to)
    east, west = border_cols(adjoint, transport_rates)
    east, west = corners(east, west, before, after, lats)
    w_in = lax.ppermute(east, "lon", east_to)
    e_in = lax.ppermute(west, "lon", west_to)
    blocks = regions // LANES
    hot, zc, half, w1 = tables(region_local, cell_weight, polar_rows, tile_regions.shape[1], blocks)
    where = places(tile_regions, own_rows)
    f1, mids = first_step(lats, adjoint, transport_rates, before, after, up, down, trc, lev, rows)
    lam, level0, row_sums = transport(
        lats, f1, mids, transport_rates, w_in, e_in, east, west, before, after, trc, lev, rows)

    if lons <= 4:
        parts = [row_sums] + [lax.ppermute(row_sums, "lon", partners(lons, k)) for k in range(1, lons)]
    else:
        got = lax.all_to_all(
            jnp.broadcast_to(row_sums[None], (lons,) + row_sums.shape), "lon", 0, 0, tiled=True)
        parts = [jnp.sum(got, axis=0)]
    s1 = local_sums(level0, w1, hot)
    zonal, copies = regional(parts, s1, zc, trc, devices, cols * lons, blocks)
    sums = lax.all_to_all(copies, AXES, 0, 0, tiled=True)
    sums = sums.reshape(-1, sums.shape[2])
    adjoint_out = filtered(lam, zonal, half, trc, lev).reshape(adjoint.shape)
    far_cov = lax.ppermute(far_columns(covariance), AXES, top)
    base, other = base_product(have, theirs, covariance, far_cov, turn, grad_in.shape[1])
    more = lax.ppermute(other, AXES, top)
    precond = finish(week_index, sums, where, covariance, base, more, trc)
    return adjoint_out, precond


def solution(mesh):
    in_specs = (
        P(None, None, "lat", "lon"),
        P(None, None, "lat", "lon"),
        P("lat", "lon"),
        P("lat", "lon"),
        P(),
        P("lat"),
        P(),
        P(("lat", "lon"), None),
        P(("lat", "lon"), None),
    )
    out_specs = (P(None, None, "lat", "lon"), P(("lat", "lon"), None))
    return jax.shard_map(shards, mesh=mesh, in_specs=in_specs, out_specs=out_specs, check_vma=False)
```
